512 devices in a mesh: section: 8 (over y, core), shard: 64 (over z, x).
Axes of the slice: x: 4, y: 4, z: 16, core: 2. Of those that a mesh axis runs over, the one named last changes fastest.
Arguments:
- features: bfloat16 [8, 16384, 512], P(None, 'shard'), may hold values from -0.029907227 to 0.029907227
- labels: int32 [8, 16384], P(None, 'shard'), may hold values from 0 to 3
- label_table: float32 [4, 512], replicated, may hold values from -0.01 to 0.01
- tiles: bfloat16 [8, 384, 128, 128], P(None, 'shard'), may hold values from -1 to 1
- tile_rows: int32 [8, 384], P(None, 'shard'), may hold values from 0 to 127, as said below
- tile_cols: int32 [8, 384], P(None, 'shard'), may hold values from 0 to 127, as said below
- tile_live: int32 [8, 64], P(None, 'shard'), may hold values from 2 to 6, as said below
- weights: bfloat16 [8, 512, 512], P('section'), may hold values from -0.25 to 0.25
- gains: bfloat16 [8, 512], P('section'), may hold values from 0 to 1
- head_weight: float32 [512], replicated, may hold values from -0.75 to 0.75
Outputs:
- outcome: float32 [8, 16384], P('section', 'shard')
The draws below stay inside these ranges and needn't reach their ends.
Inputs may be any that keep to these rules, and one draw needn't show every extreme that they name: `tile_rows`: slot k of shard j has a row block from j * 2 - 1 to (j + 1) * 2. `tile_cols`: slot k of shard j has a column block of that shard's own nodes, j * 2 to (j + 1) * 2 - 1; where its row block is j * 2 - 1 the column block is j * 2, and where its row block is (j + 1) * 2 the column block is (j + 1) * 2 - 1. `tile_live`: in every graph group some shard has all 6 slots live.
All inputs are finite; a program needn't handle non-finite values.
Results may differ from the reference program's by a relative error of at most 0.02.
Values may be sent and summed in bfloat16 or wider, within the bound.
A program may use at most 64 MiB of HBM per device.

```python
import jax
import jax.numpy as jnp
from jax import lax

D = 512
LABELS = 4
TILE = 128
TILES = 6
ROWS_DEV = 256
MB_SECTION = 1
MB = 8
NODES = 16384
BLOCKS = 128
SLOTS = 384
N_SECTION = 8


def tile_layout(key):
    per_rows = ROWS_DEV // TILE
    shard_count = NODES // ROWS_DEV
    key_place, key_column, key_count, key_heavy, key_pick = jax.random.split(jax.random.fold_in(key, 7), 5)
    position = jax.random.randint(key_place, (MB, shard_count, TILES), 0, per_rows + 2)
    position = position.at[:, :, 0].set(0).at[:, :, 1].set(per_rows + 1)
    shard_ids = jnp.arange(shard_count, dtype=jnp.int32)[None, :, None]
    row_blocks = jnp.clip(shard_ids * per_rows - 1 + position, 0, BLOCKS - 1)
    col_offset = jax.random.randint(key_column, (MB, shard_count, TILES), 0, per_rows)
    col_offset = jnp.where(position == 0, 0, jnp.where(position == per_rows + 1, per_rows - 1, col_offset))
    col_blocks = shard_ids * per_rows + col_offset
    base_count = jax.random.randint(key_count, (MB, shard_count), 2, 4)
    busy_shard = jax.random.randint(key_heavy, (MB, shard_count), 0, 8) == 0
    chosen = jax.random.randint(key_pick, (MB, 1), 0, shard_count)
    forced_shard = jnp.arange(shard_count, dtype=jnp.int32)[None, :] == chosen
    counts = jnp.where(busy_shard | forced_shard, TILES, jnp.minimum(base_count, TILES)).astype(jnp.int32)
    return (row_blocks.reshape(MB, SLOTS).astype(jnp.int32), col_blocks.reshape(MB, SLOTS).astype(jnp.int32), counts, position.reshape(MB, SLOTS).astype(jnp.int32))


def draw_tile_rows(key, part):
    return tile_layout(key)[0]


def draw_tile_cols(key, part):
    return tile_layout(key)[1]


def draw_tile_live(key, part):
    return tile_layout(key)[2]


def draw_tiles(key, part):
    position = tile_layout(key)[3]
    toward_lower = position == 0
    array_shape = (MB, SLOTS, TILE, TILE)
    value_key = jax.random.fold_in(key, 11)
    sample = jnp.clip(jax.random.normal(value_key, array_shape, jnp.float32), -5.0, 5.0)
    factor = jnp.where(toward_lower, 0.15, 1.0).astype(jnp.float32)
    values = sample * factor[:, :, None, None] * (2.0 * TILE) ** (-0.5)
    return values.astype(jnp.bfloat16)


def draw_gains(key, part):
    sections = MB // MB_SECTION
    layer_ids = jnp.arange(sections, dtype=jnp.float32)[:, None]
    base_gain = 0.5 * jnp.exp(jnp.log(1.7) * (layer_ids - (sections - 1)))
    gain_key = jax.random.fold_in(key, 13)
    spread = jnp.exp(jax.random.uniform(gain_key, (sections, D), jnp.float32, -0.5, 0.5))
    return (base_gain * spread).astype(jnp.bfloat16)


def set_ends(drawn, key, least, high):
    index_at = [jax.random.randint(jax.random.fold_in(key, axis), (), 0, length) for axis, length in enumerate(drawn.shape)]
    longest = drawn.shape.index(max(drawn.shape))
    beside = index_at[:longest] + [(index_at[longest] + 1) % drawn.shape[longest]] + index_at[longest + 1:]
    return drawn.at[tuple(index_at)].set(least).at[tuple(beside)].set(high)


def block_scale(stream_key, shape, shards, smallest, largest):
    level = 1.0
    for axis_at, shards_of in shards:
        draws = jax.random.uniform(jax.random.fold_in(jax.random.fold_in(stream_key, 6), axis_at), (shards_of,), jnp.float32, smallest / len(shards), largest / len(shards))
        level = level * jnp.repeat(jnp.exp(draws), shape[axis_at] // shards_of).reshape((-1,) + (1,) * (len(shape) - 1 - axis_at))
    return level


def normal_values(rng, dims, scale, reach, cuts=(), held_as=jnp.bfloat16):
    factor_of = block_scale(rng, dims, cuts, -0.22, 0.18) if cuts else 1.0
    values = jax.random.normal(rng, dims, jnp.float32) * scale * factor_of
    return jnp.minimum(jnp.maximum(values, -reach), reach).astype(held_as)


def setup_inputs(seed: int = 0) -> dict:
    streams_of = jax.random.split(jax.random.key(seed), 11)
    return {
        "features": normal_values(streams_of[0], (MB, NODES, D), 0.005, 0.029907227, ((1, 64),)),
        "labels": set_ends(jax.random.randint(streams_of[1], (MB, NODES), 0, LABELS), jax.random.fold_in(streams_of[1], 1), 0, LABELS - 1).astype(jnp.int32),
        "label_table": jnp.clip(jax.random.uniform(streams_of[2], (LABELS, D), jnp.float32, -0.01, 0.01), -0.01, 0.01),
        "tiles": draw_tiles(jax.random.fold_in(streams_of[10], 71), 0),
        "tile_rows": draw_tile_rows(jax.random.fold_in(streams_of[10], 71), 0),
        "tile_cols": draw_tile_cols(jax.random.fold_in(streams_of[10], 71), 0),
        "tile_live": draw_tile_live(jax.random.fold_in(streams_of[10], 71), 0),
        "weights": normal_values(streams_of[7], (N_SECTION, D, D), D ** -0.5, 0.25, ((0, 8),)),
        "gains": draw_gains(jax.random.fold_in(streams_of[10], 71), 0),
        "head_weight": normal_values(streams_of[9], (D,), (D // 8) ** -0.5, 0.75, (), jnp.float32),
    }


def reference(features, labels, label_table, tiles, tile_rows, tile_cols, tile_live, weights, gains, head_weight):
    slot_ids = jnp.arange(SLOTS, dtype=jnp.int32) % TILES

    def one_group(batch_index):
        labels_hot = (labels[batch_index][:, None] == jnp.arange(LABELS, dtype=jnp.int32)[None, :]).astype(jnp.float32)
        embedded = jnp.dot(labels_hot, label_table, precision=lax.Precision.HIGHEST)
        state = (features[batch_index].astype(jnp.float32) + embedded).astype(jnp.bfloat16)
        live_mask = (slot_ids < jnp.repeat(tile_live[batch_index], TILES)).astype(jnp.float32)
        group_tiles = tiles[batch_index].astype(jnp.float32)
        for layer_index in range(N_SECTION):
            block_view = state.reshape(BLOCKS, TILE, D)
            chosen_blocks = jnp.take(block_view, tile_cols[batch_index], axis=0).astype(jnp.float32)
            products = jnp.einsum('kab,kbd->kad', group_tiles, chosen_blocks, precision=lax.Precision.HIGHEST)
            products = products * live_mask[:, None, None]
            aggregate = jax.ops.segment_sum(products, tile_rows[batch_index], num_segments=BLOCKS)
            aggregate = aggregate.reshape(NODES, D).astype(jnp.bfloat16)
            projected = jnp.dot(aggregate, weights[layer_index], preferred_element_type=jnp.float32)
            scale = lax.rsqrt(lax.optimization_barrier(jnp.mean(projected * projected, axis=-1, keepdims=True)) + 1e-06)
            normed = projected * scale * gains[layer_index].astype(jnp.float32)
            state = (state.astype(jnp.float32) + jax.nn.gelu(normed)).astype(jnp.bfloat16)
        return jnp.dot(state.astype(jnp.float32), head_weight, precision=lax.Precision.HIGHEST)
    return lax.map(one_group, jnp.arange(MB, dtype=jnp.int32))
```

```python
import jax
import jax.numpy as jnp
from jax import lax
from jax.experimental import pallas as pl
from jax.experimental.pallas import tpu as pltpu
from jax.sharding import PartitionSpec as P

F32, BF16, I32 = jnp.float32, jnp.bfloat16, jnp.int32
T = 128
D = 512
HALF = 256
LAYERS = 8
SLOTS = 6
YN = 4
XN = 4
CHAIN = 32


def dot(a, b):
    return jnp.dot(a, b, preferred_element_type=F32)


def remote(src, dst, send, recv, dev):
    return pltpu.make_async_remote_copy(
        src_ref=src,
        dst_ref=dst,
        send_sem=send,
        recv_sem=recv,
        device_id=dev,
        device_id_type=pl.DeviceIdType.MESH,
    )


def along(z, hi, f):
    return 2 * hi + jnp.where(lax.rem(z + hi, 2) == 0, f, 1 - f)


def kernel(
    feat, labels, table, tiles, rows, cols, live, w, gains, head,
    out,
    fbuf, tbuf, mown, mbuf, gown, gbuf, wbuf, sbuf, hs, hn, acat, aout, ain, own, obuf, rbuf,
    red_s, red_r, wloc, os_s, gos_s, w_r, g_r, rel_s, grel_s, fw_s, gfw_s, a_s, a_r, h_s, h_r,
    o_s, o_r, stage,
):
    sec = lax.axis_index("section")
    sh = lax.axis_index("shard")
    y, c = lax.div(sec, 2), lax.rem(sec, 2)
    z, x = lax.div(sh, XN), lax.rem(sh, XN)
    hi = lax.div(x, 2)
    xl = lax.rem(x, 2)
    f = jnp.where(lax.rem(z + hi, 2) == 0, xl, 1 - xl)
    g = 2 * y + hi
    t = XN * z + 2 * f + c
    place = 2 * z + f
    sib = (2 * y + 1 - c, sh)
    other = lax.rem(place + 2 * c - 1 + CHAIN, CHAIN)
    oz, of = lax.div(other, 2), lax.rem(other, 2)
    nb = (2 * y + 1 - c, XN * oz + along(oz, hi, of))
    up = lax.rem(y + 1, YN)
    down = lax.rem(y + YN - 1, YN)
    opp = lax.rem(y + 2, YN)
    yp = (2 * up + c, sh)
    ym = (2 * down + c, sh)
    to_x = along(z, c, lax.div(x, 2))
    to_sec = 2 * y + lax.rem(x, 2)
    to = (to_sec, XN * z + to_x)
    stay = (to_sec == sec) & (to_x == x)
    back = (g, t)
    moves = jnp.logical_not(stay)

    mown[...] = jnp.zeros((8, 256), I32)
    mown[0:1, :] = labels[pl.ds(sec, 1), :]
    mown[1:2, 0:SLOTS] = rows[pl.ds(sec, 1), :]
    mown[2:3, 0:SLOTS] = cols[pl.ds(sec, 1), :]
    mown[3:4, 0:1] = live[pl.ds(sec, 1), :]
    gown[...] = jnp.broadcast_to(gains[...].astype(F32), (8, D))

    barrier = pltpu.get_barrier_semaphore()
    for dev in (sib, nb, yp, ym):
        pl.semaphore_signal(barrier, inc=1, device_id=dev, device_id_type=pl.DeviceIdType.MESH)

    @pl.when(moves)
    def _():
        for dev in (to, back):
            pl.semaphore_signal(barrier, inc=1, device_id=dev, device_id_type=pl.DeviceIdType.MESH)
        pl.semaphore_wait(barrier, 6)

    @pl.when(stay)
    def _():
        pl.semaphore_wait(barrier, 4)

    red = ((mown, mbuf), (tiles.at[sec], tbuf), (feat.at[sec], fbuf))

    @pl.when(moves)
    def _():
        for i, (src, dst) in enumerate(red):
            remote(src, dst, red_s.at[i], red_r.at[i], to).start()

    @pl.when(stay)
    def _():
        for i, (src, dst) in enumerate(red):
            pltpu.make_async_copy(src, dst, red_r.at[i]).start()

    def half(h):
        return pl.ds(h * HALF, HALF)

    def own_weight(k, h, dev):
        return remote(w.at[0, half(h)], wbuf.at[sec, half(h)], os_s.at[k, h], w_r.at[sec, h], dev)

    def own_gain(k, dev):
        return remote(gown, gbuf.at[sec], gos_s.at[k], g_r.at[sec], dev)

    def forward(l, h, send, dev):
        return remote(wbuf.at[l, half(h)], wbuf.at[l, half(h)], send, w_r.at[l, h], dev)

    def forward_gain(l, send, dev):
        return remote(gbuf.at[l], gbuf.at[l], send, g_r.at[l], dev)

    def await_weight(l, h):
        pltpu.make_async_copy(wbuf.at[l, half(h)], wbuf.at[l, half(h)], w_r.at[l, h]).wait()

    def await_gain(l):
        pltpu.make_async_copy(gbuf.at[l], gbuf.at[l], g_r.at[l]).wait()

    lm, lp, l2 = 2 * down + c, 2 * up + c, 2 * opp + c

    def to_chips():
        own_gain(0, yp).start()
        own_gain(1, ym).start()
        own_weight(0, 0, yp).start()
        own_weight(1, 1, ym).start()
        own_weight(0, 1, yp).start()
        own_weight(1, 0, ym).start()

    def near():
        await_gain(lm)
        await_weight(lm, 0)
        forward_gain(lm, grel_s.at[0], yp).start()
        forward(lm, 0, rel_s.at[0], yp).start()
        forward_gain(lm, gfw_s.at[lm], sib).start()
        forward(lm, 0, fw_s.at[lm, 0], sib).start()
        await_weight(lp, 1)
        forward(lp, 1, rel_s.at[1], ym).start()
        forward(lp, 1, fw_s.at[lp, 1], sib).start()
        await_weight(lm, 1)
        forward(lm, 1, fw_s.at[lm, 1], sib).start()
        await_gain(lp)
        await_weight(lp, 0)
        forward_gain(lp, gfw_s.at[lp], sib).start()
        forward(lp, 0, fw_s.at[lp, 0], sib).start()

    def far():
        await_gain(l2)
        await_weight(l2, 0)
        forward_gain(l2, gfw_s.at[l2], sib).start()
        forward(l2, 0, fw_s.at[l2, 0], sib).start()
        await_weight(l2, 1)
        forward(l2, 1, fw_s.at[l2, 1], sib).start()

    own_local = pltpu.make_async_copy(w.at[0], wbuf.at[sec], wloc)
    own_local.start()
    gbuf[sec] = gown[...]

    @pl.when(c == 0)
    def _():
        to_chips()

    own_gain(2, sib).start()
    own_weight(2, 0, sib).start()
    own_weight(2, 1, sib).start()

    def await_red(i, dst):
        pltpu.make_async_copy(dst, dst, red_r.at[i]).wait()

    await_red(0, mbuf)
    await_red(1, tbuf)
    trow, tcol, tlive = mbuf[1:2, 0:T], mbuf[2:3, 0:T], mbuf[3:4, 0:1]
    alive = lax.broadcasted_iota(I32, (1, T), 1) < tlive

    def dense(r, cc):
        coef = jnp.where((trow == r) & (tcol == cc) & alive, 1.0, 0.0).astype(F32)
        total = coef[:, 0:1] * tbuf[0].astype(F32)
        for k in range(1, SLOTS):
            total = total + coef[:, k : k + 1] * tbuf[k].astype(F32)
        return total.astype(BF16)

    inner, outer = 2 * t + 1 - c, 2 * t + c
    aout[0] = dense(2 * t + 2 - 3 * c, inner)
    aout[1] = dense(2 * t - 1 + 3 * c, outer)
    rim0 = remote(aout.at[0], ain.at[0], a_s.at[0], a_r.at[0], sib)
    rim1 = remote(aout.at[1], ain.at[1], a_s.at[1], a_r.at[1], nb)
    rim0.start()
    rim1.start()

    await_red(2, fbuf)
    kinds = lax.broadcasted_iota(I32, (T, 256), 0)
    hot = jnp.where(kinds == mbuf[0:1, :], 1.0, 0.0).astype(F32).T
    embedded = hot[:, 0:1] * table[0:1, :]
    for k in range(1, 4):
        embedded = embedded + hot[:, k : k + 1] * table[k : k + 1, :]
    first = (fbuf[...].astype(F32) + embedded).astype(BF16)
    sbuf[0, pl.ds(pl.multiple_of((1 - c) * T, T), T), :] = first[0:T]
    sbuf[0, pl.ds(pl.multiple_of(c * T, T), T), :] = first[T : 2 * T]

    def send_inner(slot):
        return remote(sbuf.at[slot, pl.ds(0, T)], hs.at[slot], h_s.at[0, slot], h_r.at[0, slot], sib)

    def send_outer(slot):
        return remote(sbuf.at[slot, pl.ds(T, T)], hn.at[slot], h_s.at[1, slot], h_r.at[1, slot], nb)

    send_outer(0).start()
    send_inner(0).start()

    acat[0:T, 0:T] = dense(inner, inner)
    acat[0:T, T : 2 * T] = dense(inner, outer)
    acat[T : 2 * T, 0:T] = dense(outer, inner)
    acat[T : 2 * T, T : 2 * T] = dense(outer, outer)

    @pl.when(c == 0)
    def _():
        near()
        own_weight(0, 0, yp).wait_send()
        own_weight(0, 1, yp).wait_send()
        own_weight(1, 0, ym).wait_send()
        own_weight(1, 1, ym).wait_send()
        pl.semaphore_signal(stage, inc=1, device_id=sib, device_id_type=pl.DeviceIdType.MESH)
        far()

    @pl.when(c == 1)
    def _():
        pl.semaphore_wait(stage, 1)
        to_chips()

    own_local.wait()
    rim0.wait()
    rim1.wait()

    def layer(l, carry):
        slot = lax.rem(l, 2)
        nxt = 1 - slot

        own[...] = dot(acat[...], sbuf[slot])

        @pl.when((c == 1) & (l == 1))
        def _():
            near()
            far()

        @pl.when(lax.rem(l, 2) != c)
        def _():
            await_gain(l)
            await_weight(l, 0)
            await_weight(l, 1)

        gain = gbuf[l][0:1, :]

        def block(p, halo):
            rs = pl.ds(p * T, T)
            aggregate = (own[rs, :] + dot(ain[p], halo[slot])).astype(BF16)
            projected = dot(aggregate, wbuf[l])
            scale = lax.rsqrt(jnp.mean(projected * projected, axis=-1, keepdims=True) + 1e-6)
            normed = projected * scale * gain
            sbuf[nxt, rs, :] = (sbuf[slot, rs, :].astype(F32) + jax.nn.gelu(normed)).astype(BF16)

        send_inner(slot).wait()
        block(0, hs)

        @pl.when(l < LAYERS - 1)
        def _():
            send_inner(nxt).start()

        send_outer(slot).wait()
        block(1, hn)

        @pl.when(l < LAYERS - 1)
        def _():
            send_outer(nxt).start()

        return carry

    lax.fori_loop(0, LAYERS, layer, 0)

    last = sbuf[0]
    weight = jnp.broadcast_to(head[...], (8, D))
    top = weight.astype(BF16)
    rest = weight - top.astype(F32)
    mid = rest.astype(BF16)
    low = (rest - mid.astype(F32)).astype(BF16)

    def against(part):
        return lax.dot_general(part, last, (((1,), (1,)), ((), ())), preferred_element_type=F32)

    result = against(top) + against(mid) + against(low)
    obuf[1 - c] = result[:, 0:T]
    obuf[c] = result[:, T : 2 * T]

    @pl.when(moves)
    def _():
        give = remote(obuf, rbuf, o_s, o_r, back)
        give.start()
        give.wait_send()

    @pl.when(stay)
    def _():
        pltpu.make_async_copy(obuf, rbuf, o_r).start()

    for k, dev in enumerate((yp, ym, sib)):
        own_gain(k, dev).wait_send()

    @pl.when(c == 1)
    def _():
        for k, dev in enumerate((yp, ym)):
            for h in range(2):
                own_weight(k, h, dev).wait_send()

    own_weight(2, 0, sib).wait_send()
    own_weight(2, 1, sib).wait_send()
    forward_gain(lm, grel_s.at[0], yp).wait_send()
    forward(lm, 0, rel_s.at[0], yp).wait_send()
    forward(lp, 1, rel_s.at[1], ym).wait_send()
    for l in (lm, lp, l2):
        forward_gain(l, gfw_s.at[l], sib).wait_send()
        forward(l, 0, fw_s.at[l, 0], sib).wait_send()
        forward(l, 1, fw_s.at[l, 1], sib).wait_send()

    @pl.when(moves)
    def _():
        for i, (src, dst) in enumerate(red):
            remote(src, dst, red_s.at[i], red_r.at[i], to).wait_send()

    pltpu.make_async_copy(rbuf, rbuf, o_r).wait()
    out[0:1, 0:T] = rbuf[0, 0:1, :]
    out[0:1, T : 2 * T] = rbuf[1, 0:1, :]


def body(features, labels, label_table, tiles, tile_rows, tile_cols, tile_live, weights, gains, head_weight):
    vmem = pl.BlockSpec(memory_space=pltpu.VMEM)
    far = pl.BlockSpec(memory_space=pl.ANY)
    dma = pltpu.SemaphoreType.DMA
    return pl.pallas_call(
        kernel,
        out_shape=jax.ShapeDtypeStruct((1, 2 * T), F32),
        in_specs=[far, vmem, vmem, far, vmem, vmem, vmem, far, vmem, vmem],
        out_specs=vmem,
        scratch_shapes=[
            pltpu.VMEM((2 * T, D), BF16),
            pltpu.VMEM((SLOTS, T, T), BF16),
            pltpu.VMEM((8, 256), I32),
            pltpu.VMEM((8, 256), I32),
            pltpu.VMEM((8, D), F32),
            pltpu.VMEM((LAYERS, 8, D), F32),
            pltpu.VMEM((LAYERS, D, D), BF16),
            pltpu.VMEM((2, 2 * T, D), BF16),
            pltpu.VMEM((2, T, D), BF16),
            pltpu.VMEM((2, T, D), BF16),
            pltpu.VMEM((2 * T, 2 * T), BF16),
            pltpu.VMEM((2, T, T), BF16),
            pltpu.VMEM((2, T, T), BF16),
            pltpu.VMEM((2 * T, D), F32),
            pltpu.VMEM((2, 8, T), F32),
            pltpu.VMEM((2, 8, T), F32),
            dma((3,)),
            dma((3,)),
            dma,
            dma((3, 2)),
            dma((3,)),
            dma((LAYERS, 2)),
            dma((LAYERS,)),
            dma((2,)),
            dma((1,)),
            dma((LAYERS, 2)),
            dma((LAYERS,)),
            dma((2,)),
            dma((2,)),
            dma((2, 2)),
            dma((2, 2)),
            dma,
            dma,
            pltpu.SemaphoreType.REGULAR,
        ],
        compiler_params=pltpu.CompilerParams(collective_id=0, has_side_effects=True),
    )(
        features, labels, label_table, tiles, tile_rows, tile_cols, tile_live, weights, gains,
        head_weight.reshape(1, D),
    )


def solution(mesh):
    return jax.shard_map(
        body,
        mesh=mesh,
        in_specs=(
            P(None, "shard", None),
            P(None, "shard"),
            P(),
            P(None, "shard", None, None),
            P(None, "shard"),
            P(None, "shard"),
            P(None, "shard"),
            P("section", None, None),
            P("section", None),
            P(),
        ),
        out_specs=P("section", "shard"),
        check_vma=False,
    )
```

```python
import jax
import jax.numpy as jnp
from jax import lax
from jax.experimental import pallas as pl
from jax.experimental.pallas import tpu as pltpu
from jax.sharding import PartitionSpec as P

F32, BF16, I32 = jnp.float32, jnp.bfloat16, jnp.int32
T = 128
D = 512
HALF = 256
LAYERS = 8
SLOTS = 6
YN = 4
XN = 4
CHAIN = 32


def dot(a, b):
    return jnp.dot(a, b, preferred_element_type=F32)


def remote(src, dst, send, recv, dev):
    return pltpu.make_async_remote_copy(
        src_ref=src,
        dst_ref=dst,
        send_sem=send,
        recv_sem=recv,
        device_id=dev,
        device_id_type=pl.DeviceIdType.MESH,
    )


def along(z, hi, f):
    return 2 * hi + jnp.where(lax.rem(z + hi, 2) == 0, f, 1 - f)


def kernel(
    feat, labels, table, tiles, rows, cols, live, w, gains, head,
    out,
    fbuf, tbuf, mown, mbuf, gown, gbuf, wbuf, sbuf, hs, hn, acat, aout, ain, anb, own, pre, hb,
    obuf, rbuf,
    red_s, red_r, wloc, os_s, gos_s, w_r, g_r, rel_s, grel_s, fw_s, gfw_s, a_s, a_r, h_s, h_r,
    n_s, n_r, o_s, o_r,
):
    sec = lax.axis_index("section")
    sh = lax.axis_index("shard")
    y, c = lax.div(sec, 2), lax.rem(sec, 2)
    z, x = lax.div(sh, XN), lax.rem(sh, XN)
    hi = lax.div(x, 2)
    xl = lax.rem(x, 2)
    f = jnp.where(lax.rem(z + hi, 2) == 0, xl, 1 - xl)
    g = 2 * y + hi
    t = XN * z + 2 * f + c
    place = 2 * z + f
    sib = (2 * y + 1 - c, sh)
    other = place + 2 * c - 1
    joined = (other >= 0) & (other < CHAIN)
    other = lax.rem(other + CHAIN, CHAIN)
    oz, of = lax.div(other, 2), lax.rem(other, 2)
    nb = (2 * y + 1 - c, XN * oz + along(oz, hi, of))
    up = lax.rem(y + 1, YN)
    down = lax.rem(y + YN - 1, YN)
    opp = lax.rem(y + 2, YN)
    yp = (2 * up + c, sh)
    ym = (2 * down + c, sh)
    to_x = along(z, c, lax.div(x, 2))
    to_sec = 2 * y + lax.rem(x, 2)
    to = (to_sec, XN * z + to_x)
    stay = (to_sec == sec) & (to_x == x)
    back = (g, t)
    moves = jnp.logical_not(stay)

    mown[...] = jnp.zeros((8, 256), I32)
    mown[0:1, :] = labels[pl.ds(sec, 1), :]
    mown[1:2, 0:SLOTS] = rows[pl.ds(sec, 1), :]
    mown[2:3, 0:SLOTS] = cols[pl.ds(sec, 1), :]
    mown[3:4, 0:8] = live[...]
    gown[...] = jnp.broadcast_to(gains[...].astype(F32), (8, D))

    barrier = pltpu.get_barrier_semaphore()

    def greet(*devs):
        for dev in devs:
            pl.semaphore_signal(barrier, inc=1, device_id=dev, device_id_type=pl.DeviceIdType.MESH)

    greet(sib, yp, ym)

    @pl.when(joined)
    def _():
        greet(nb)

    @pl.when(moves)
    def _():
        greet(to, back)

    pl.semaphore_wait(barrier, 3 + jnp.where(joined, 1, 0) + jnp.where(moves, 2, 0))

    red = ((mown, mbuf), (tiles.at[sec], tbuf), (feat.at[sec], fbuf))

    @pl.when(moves)
    def _():
        for i, (src, dst) in enumerate(red):
            remote(src, dst, red_s.at[i], red_r.at[i], to).start()

    @pl.when(stay)
    def _():
        for i, (src, dst) in enumerate(red):
            pltpu.make_async_copy(src, dst, red_r.at[i]).start()

    def half(h):
        return pl.ds(h * HALF, HALF)

    def own_weight(k, h, dev):
        return remote(w.at[0, half(h)], wbuf.at[sec, half(h)], os_s.at[k, h], w_r.at[sec, h], dev)

    def own_gain(k, dev):
        return remote(gown, gbuf.at[sec], gos_s.at[k], g_r.at[sec], dev)

    def forward(l, h, send, dev):
        return remote(wbuf.at[l, half(h)], wbuf.at[l, half(h)], send, w_r.at[l, h], dev)

    def forward_gain(l, send, dev):
        return remote(gbuf.at[l], gbuf.at[l], send, g_r.at[l], dev)

    def await_weight(l, h):
        pltpu.make_async_copy(wbuf.at[l, half(h)], wbuf.at[l, half(h)], w_r.at[l, h]).wait()

    def await_gain(l):
        pltpu.make_async_copy(gbuf.at[l], gbuf.at[l], g_r.at[l]).wait()

    lm, lp, l2 = 2 * down + c, 2 * up + c, 2 * opp + c

    def to_chips():
        own_gain(0, yp).start()
        own_gain(1, ym).start()
        own_weight(0, 0, yp).start()
        own_weight(1, 1, ym).start()
        own_weight(0, 1, yp).start()
        own_weight(1, 0, ym).start()

    def near_first():
        await_gain(lm)
        await_weight(lm, 0)
        forward_gain(lm, grel_s.at[0], yp).start()
        forward(lm, 0, rel_s.at[0], yp).start()
        forward_gain(lm, gfw_s.at[lm], sib).start()
        forward(lm, 0, fw_s.at[lm, 0], sib).start()
        await_weight(lp, 1)
        forward(lp, 1, rel_s.at[1], ym).start()
        forward(lp, 1, fw_s.at[lp, 1], sib).start()

    def near_second():
        await_weight(lm, 1)
        forward(lm, 1, fw_s.at[lm, 1], sib).start()
        await_gain(lp)
        await_weight(lp, 0)
        forward_gain(lp, gfw_s.at[lp], sib).start()
        forward(lp, 0, fw_s.at[lp, 0], sib).start()

    def far():
        await_gain(l2)
        await_weight(l2, 0)
        forward_gain(l2, gfw_s.at[l2], sib).start()
        forward(l2, 0, fw_s.at[l2, 0], sib).start()
        await_weight(l2, 1)
        forward(l2, 1, fw_s.at[l2, 1], sib).start()

    own_local = pltpu.make_async_copy(w.at[0], wbuf.at[sec], wloc)
    own_local.start()
    gbuf[sec] = gown[...]

    to_chips()
    own_gain(2, sib).start()
    own_weight(2, 0, sib).start()
    own_weight(2, 1, sib).start()

    def await_red(i, dst):
        pltpu.make_async_copy(dst, dst, red_r.at[i]).wait()

    await_red(0, mbuf)
    await_red(1, tbuf)
    trow, tcol = mbuf[1:2, 0:T], mbuf[2:3, 0:T]
    lane = lax.broadcasted_iota(I32, (1, T), 1)
    tlive = jnp.sum(jnp.where(lane == g, mbuf[3:4, 0:T], 0), axis=1, keepdims=True)
    alive = lane < tlive

    def dense(r, cc):
        coef = jnp.where((trow == r) & (tcol == cc) & alive, 1.0, 0.0).astype(F32)
        total = coef[:, 0:1] * tbuf[0].astype(F32)
        for k in range(1, SLOTS):
            total = total + coef[:, k : k + 1] * tbuf[k].astype(F32)
        return total.astype(BF16)

    inner, outer = 2 * t + 1 - c, 2 * t + c
    acat[T : 2 * T, 0:T] = dense(outer, inner)
    acat[T : 2 * T, T : 2 * T] = dense(outer, outer)
    aout[1] = dense(2 * t - 1 + 3 * c, outer)
    aout[0] = dense(2 * t + 2 - 3 * c, inner)
    rim0 = remote(aout.at[0], ain.at[0], a_s.at[0], a_r.at[0], sib)
    rim1 = remote(aout.at[1], ain.at[1], a_s.at[1], a_r.at[1], nb)
    rim2 = remote(acat.at[pl.ds(T, T)], anb, a_s.at[2], a_r.at[2], nb)
    rim0.start()

    @pl.when(joined)
    def _():
        rim1.start()
        rim2.start()

    @pl.when(jnp.logical_not(joined))
    def _():
        ain[1] = jnp.zeros((T, T), BF16)
        anb[...] = jnp.zeros((T, 2 * T), BF16)
        hn[...] = jnp.zeros((2, 2 * T, D), BF16)

    acat[0:T, 0:T] = dense(inner, inner)
    acat[0:T, T : 2 * T] = dense(inner, outer)
    near_first()

    await_red(2, fbuf)
    kinds = lax.broadcasted_iota(I32, (T, 256), 0)
    hot = jnp.where(kinds == mbuf[0:1, :], 1.0, 0.0).astype(F32).T
    embedded = hot[:, 0:1] * table[0:1, :]
    for k in range(1, 4):
        embedded = embedded + hot[:, k : k + 1] * table[k : k + 1, :]
    first = (fbuf[...].astype(F32) + embedded).astype(BF16)
    sbuf[0, pl.ds(pl.multiple_of((1 - c) * T, T), T), :] = first[0:T]
    sbuf[0, pl.ds(pl.multiple_of(c * T, T), T), :] = first[T : 2 * T]

    inn, out_ = pl.ds(0, T), pl.ds(T, T)

    def send_inner(level):
        k = lax.rem(level, 2)
        return remote(sbuf.at[lax.rem(level, 4), inn], hs.at[k], h_s.at[k], h_r.at[k], sib)

    def send_across(step, p):
        k = lax.rem(step, 2)
        rs = pl.ds(p * T, T)
        return remote(sbuf.at[2 * k, rs], hn.at[k, rs], n_s.at[k, p], n_r.at[k, p], nb)

    def cross(step, p, what):
        @pl.when(joined)
        def _():
            if what == "go":
                send_across(step, p).start()
            else:
                send_across(step, p).wait()

    send_inner(0).start()
    cross(0, 0, "go")
    cross(0, 1, "go")
    near_second()
    far()
    own_local.wait()
    rim0.wait()

    @pl.when(joined)
    def _():
        rim1.wait()
        rim2.wait()

    def other_weight(l):
        await_gain(l)
        await_weight(l, 0)
        await_weight(l, 1)

    def update(l, aggregate, before):
        projected = dot(aggregate.astype(BF16), wbuf[l])
        scale = lax.rsqrt(jnp.mean(projected * projected, axis=-1, keepdims=True) + 1e-6)
        normed = projected * scale * gbuf[l][0:1, :]
        return (before.astype(F32) + jax.nn.gelu(normed)).astype(BF16)

    def two_layers(i, carry):
        l = 2 * i
        a, b, n = 2 * lax.rem(i, 2), 2 * lax.rem(i, 2) + 1, lax.rem(2 * i + 2, 4)
        k = lax.rem(i, 2)

        own[...] = dot(acat[...], sbuf[a])

        @pl.when(c == 1)
        def _():
            other_weight(l)

        send_inner(l).wait()
        sbuf[b, inn, :] = update(l, own[inn, :] + dot(ain[0], hs[0]), sbuf[a, inn, :])
        send_inner(l + 1).start()

        cross(i, 0, "take")
        pre[...] = dot(aout[1], sbuf[a, out_, :]) + dot(anb[:, 0:T], hn[k, inn, :])

        @pl.when(c == 0)
        def _():
            other_weight(l + 1)

        cross(i, 1, "take")
        sbuf[b, out_, :] = update(l, own[out_, :] + dot(ain[1], hn[k, out_, :]), sbuf[a, out_, :])
        send_inner(l + 1).wait()
        sbuf[n, inn, :] = update(
            l + 1, dot(acat[inn, :], sbuf[b]) + dot(ain[0], hs[1]), sbuf[b, inn, :]
        )

        @pl.when(i < LAYERS // 2 - 1)
        def _():
            cross(i + 1, 0, "go")
            send_inner(l + 2).start()

        hb[...] = update(
            l, pre[...] + dot(anb[:, T : 2 * T], hn[k, out_, :]), hn[k, out_, :]
        )
        sbuf[n, out_, :] = update(
            l + 1, dot(acat[out_, :], sbuf[b]) + dot(ain[1], hb[...]), sbuf[b, out_, :]
        )

        @pl.when(i < LAYERS // 2 - 1)
        def _():
            cross(i + 1, 1, "go")

        return carry

    lax.fori_loop(0, LAYERS // 2, two_layers, 0)

    last = sbuf[0]
    weight = jnp.broadcast_to(head[...], (8, D))
    top = weight.astype(BF16)
    rest = weight - top.astype(F32)
    mid = rest.astype(BF16)
    low = (rest - mid.astype(F32)).astype(BF16)

    def against(part):
        return lax.dot_general(part, last, (((1,), (1,)), ((), ())), preferred_element_type=F32)

    result = against(top) + against(mid) + against(low)
    obuf[1 - c] = result[:, 0:T]
    obuf[c] = result[:, T : 2 * T]

    @pl.when(moves)
    def _():
        give = remote(obuf, rbuf, o_s, o_r, back)
        give.start()
        give.wait_send()

    @pl.when(stay)
    def _():
        pltpu.make_async_copy(obuf, rbuf, o_r).start()

    for k, dev in enumerate((yp, ym, sib)):
        own_gain(k, dev).wait_send()

    for k, dev in enumerate((yp, ym)):
        for h in range(2):
            own_weight(k, h, dev).wait_send()

    own_weight(2, 0, sib).wait_send()
    own_weight(2, 1, sib).wait_send()
    forward_gain(lm, grel_s.at[0], yp).wait_send()
    forward(lm, 0, rel_s.at[0], yp).wait_send()
    forward(lp, 1, rel_s.at[1], ym).wait_send()
    for l in (lm, lp, l2):
        forward_gain(l, gfw_s.at[l], sib).wait_send()
        forward(l, 0, fw_s.at[l, 0], sib).wait_send()
        forward(l, 1, fw_s.at[l, 1], sib).wait_send()

    @pl.when(moves)
    def _():
        for i, (src, dst) in enumerate(red):
            remote(src, dst, red_s.at[i], red_r.at[i], to).wait_send()

    pltpu.make_async_copy(rbuf, rbuf, o_r).wait()
    out[0:1, 0:T] = rbuf[0, 0:1, :]
    out[0:1, T : 2 * T] = rbuf[1, 0:1, :]


def body(features, labels, label_table, tiles, tile_rows, tile_cols, tile_live, weights, gains, head_weight):
    vmem = pl.BlockSpec(memory_space=pltpu.VMEM)
    far = pl.BlockSpec(memory_space=pl.ANY)
    dma = pltpu.SemaphoreType.DMA
    return pl.pallas_call(
        kernel,
        out_shape=jax.ShapeDtypeStruct((1, 2 * T), F32),
        in_specs=[far, vmem, vmem, far, vmem, vmem, vmem, far, vmem, vmem],
        out_specs=vmem,
        scratch_shapes=[
            pltpu.VMEM((2 * T, D), BF16),
            pltpu.VMEM((SLOTS, T, T), BF16),
            pltpu.VMEM((8, 256), I32),
            pltpu.VMEM((8, 256), I32),
            pltpu.VMEM((8, D), F32),
            pltpu.VMEM((LAYERS, 8, D), F32),
            pltpu.VMEM((LAYERS, D, D), BF16),
            pltpu.VMEM((4, 2 * T, D), BF16),
            pltpu.VMEM((2, T, D), BF16),
            pltpu.VMEM((2, 2 * T, D), BF16),
            pltpu.VMEM((2 * T, 2 * T), BF16),
            pltpu.VMEM((2, T, T), BF16),
            pltpu.VMEM((2, T, T), BF16),
            pltpu.VMEM((T, 2 * T), BF16),
            pltpu.VMEM((2 * T, D), F32),
            pltpu.VMEM((T, D), F32),
            pltpu.VMEM((T, D), BF16),
            pltpu.VMEM((2, 8, T), F32),
            pltpu.VMEM((2, 8, T), F32),
            dma((3,)),
            dma((3,)),
            dma,
            dma((3, 2)),
            dma((3,)),
            dma((LAYERS, 2)),
            dma((LAYERS,)),
            dma((2,)),
            dma((1,)),
            dma((LAYERS, 2)),
            dma((LAYERS,)),
            dma((3,)),
            dma((3,)),
            dma((2,)),
            dma((2,)),
            dma((2, 2)),
            dma((2, 2)),
            dma,
            dma,
        ],
        compiler_params=pltpu.CompilerParams(collective_id=0, has_side_effects=True),
    )(
        features, labels, label_table, tiles, tile_rows, tile_cols, tile_live.reshape(1, 8), weights, gains,
        head_weight.reshape(1, D),
    )


def solution(mesh):
    return jax.shard_map(
        body,
        mesh=mesh,
        in_specs=(
            P(None, "shard", None),
            P(None, "shard"),
            P(),
            P(None, "shard", None, None),
            P(None, "shard"),
            P(None, "shard"),
            P(None, "shard"),
            P("section", None, None),
            P("section", None),
            P(),
        ),
        out_specs=P("section", "shard"),
        check_vma=False,
    )
```

```python
import jax
import jax.numpy as jnp
from jax import lax
from jax.experimental import pallas as pl
from jax.experimental.pallas import tpu as pltpu
from jax.sharding import PartitionSpec as P

F32, BF16, I32 = jnp.float32, jnp.bfloat16, jnp.int32
T = 128
D = 512
Q = 128
QS = 4
LAYERS = 8
SLOTS = 6
YN = 4
XN = 4
CHAIN = 32


def dot(a, b):
    return jnp.dot(a, b, preferred_element_type=F32)


def remote(src, dst, send, recv, dev):
    return pltpu.make_async_remote_copy(
        src_ref=src,
        dst_ref=dst,
        send_sem=send,
        recv_sem=recv,
        device_id=dev,
        device_id_type=pl.DeviceIdType.MESH,
    )


def along(z, hi, f):
    return 2 * hi + jnp.where(lax.rem(z + hi, 2) == 0, f, 1 - f)


def kernel(
    feat, labels_h, table_h, tiles, rows_h, cols_h, live_h, w, gains_h, head_h,
    out,
    labels, table, rows, cols, live, gains, head, in_s,
    fbuf, tbuf, mown, mbuf, gown, gbuf, wbuf, sbuf, hs, hn, acat, aout, ain, anb, own, pre, hb,
    obuf, rbuf,
    red_s, red_r, wloc, os_s, gos_s, w_r, g_r, rel_s, grel_s, fw_s, gfw_s, a_s, a_r, h_s, h_r,
    n_s, n_r, o_s, o_r,
):
    sec = lax.axis_index("section")
    sh = lax.axis_index("shard")
    y, c = lax.div(sec, 2), lax.rem(sec, 2)
    z, x = lax.div(sh, XN), lax.rem(sh, XN)
    hi = lax.div(x, 2)
    xl = lax.rem(x, 2)
    f = jnp.where(lax.rem(z + hi, 2) == 0, xl, 1 - xl)
    g = 2 * y + hi
    t = XN * z + 2 * f + c
    place = 2 * z + f
    sib = (2 * y + 1 - c, sh)
    other = place + 2 * c - 1
    joined = (other >= 0) & (other < CHAIN)
    other = lax.rem(other + CHAIN, CHAIN)
    oz, of = lax.div(other, 2), lax.rem(other, 2)
    nb = (2 * y + 1 - c, XN * oz + along(oz, hi, of))
    up = lax.rem(y + 1, YN)
    down = lax.rem(y + YN - 1, YN)
    opp = lax.rem(y + 2, YN)
    yp = (2 * up + c, sh)
    ym = (2 * down + c, sh)
    to_x = along(z, c, lax.div(x, 2))
    to_sec = 2 * y + lax.rem(x, 2)
    to = (to_sec, XN * z + to_x)
    stay = (to_sec == sec) & (to_x == x)
    back = (g, t)
    moves = jnp.logical_not(stay)

    small = (
        (labels_h, labels), (rows_h, rows), (cols_h, cols), (live_h, live), (gains_h, gains),
        (table_h, table), (head_h, head),
    )
    fetches = [pltpu.make_async_copy(src, dst, in_s.at[i]) for i, (src, dst) in enumerate(small)]
    for fetch in fetches:
        fetch.start()

    barrier = pltpu.get_barrier_semaphore()

    def greet(*devs):
        for dev in devs:
            pl.semaphore_signal(barrier, inc=1, device_id=dev, device_id_type=pl.DeviceIdType.MESH)

    greet(sib, yp, ym)

    @pl.when(joined)
    def _():
        greet(nb)

    @pl.when(moves)
    def _():
        greet(to, back)

    for fetch in fetches:
        fetch.wait()

    mown[...] = jnp.zeros((8, 256), I32)
    mown[0:1, :] = labels[pl.ds(sec, 1), :]
    mown[1:2, 0:SLOTS] = rows[pl.ds(sec, 1), :]
    mown[2:3, 0:SLOTS] = cols[pl.ds(sec, 1), :]
    mown[3:4, 0:8] = live[...]
    gown[...] = jnp.broadcast_to(gains[...].astype(F32), (8, D))

    pl.semaphore_wait(barrier, 3 + jnp.where(joined, 1, 0) + jnp.where(moves, 2, 0))

    red = ((mown, mbuf), (feat.at[sec], fbuf), (tiles.at[sec], tbuf))

    @pl.when(moves)
    def _():
        for i, (src, dst) in enumerate(red):
            remote(src, dst, red_s.at[i], red_r.at[i], to).start()

    @pl.when(stay)
    def _():
        for i, (src, dst) in enumerate(red):
            pltpu.make_async_copy(src, dst, red_r.at[i]).start()

    def part(q):
        return pl.ds(q * Q, Q)

    def own_weight(k, q, dev):
        return remote(w.at[0, part(q)], wbuf.at[sec, part(q)], os_s.at[k, q], w_r.at[sec, q], dev)

    def own_gain(k, dev):
        return remote(gown, gbuf.at[sec], gos_s.at[k], g_r.at[sec], dev)

    def forward(l, q, send, dev):
        return remote(wbuf.at[l, part(q)], wbuf.at[l, part(q)], send, w_r.at[l, q], dev)

    def forward_gain(l, send, dev):
        return remote(gbuf.at[l], gbuf.at[l], send, g_r.at[l], dev)

    def await_weight(l, q):
        pltpu.make_async_copy(wbuf.at[l, part(q)], wbuf.at[l, part(q)], w_r.at[l, q]).wait()

    def await_gain(l):
        pltpu.make_async_copy(gbuf.at[l], gbuf.at[l], g_r.at[l]).wait()

    lm, lp, l2 = 2 * down + c, 2 * up + c, 2 * opp + c

    def to_chips(first):
        for q in (0, 1):
            own_weight(0, q + 2 - 2 * first, yp).start()
            own_weight(1, q + 2 * first, ym).start()

    def share(l, q):
        forward(l, q, fw_s.at[l, q], sib).start()

    def share_gain(l):
        forward_gain(l, gfw_s.at[l], sib).start()

    def relay(q):
        if q == 0:
            await_gain(lm)
            forward_gain(lm, grel_s.at[0], yp).start()
            share_gain(lm)
        await_weight(lm, q)
        forward(lm, q, rel_s.at[q], yp).start()
        await_weight(lp, q + 2)
        forward(lp, q + 2, rel_s.at[q + 2], ym).start()
        share(lm, q)
        share(lp, q + 2)

    def near():
        await_gain(lp)
        share_gain(lp)
        for q in (0, 1):
            await_weight(lm, q + 2)
            share(lm, q + 2)
            await_weight(lp, q)
            share(lp, q)

    def far():
        await_gain(l2)
        share_gain(l2)
        for q in (0, 1):
            for p in (q, q + 2):
                await_weight(l2, p)
                share(l2, p)

    own_local = pltpu.make_async_copy(w.at[0], wbuf.at[sec], wloc)
    own_local.start()
    gbuf[sec] = gown[...]

    own_gain(0, yp).start()
    own_gain(1, ym).start()
    to_chips(1)

    @pl.when(lax.rem(y, 2) == 0)
    def _():
        to_chips(0)

    own_gain(2, sib).start()
    for q in range(QS):
        own_weight(2, q, sib).start()

    def await_red(i, dst):
        pltpu.make_async_copy(dst, dst, red_r.at[i]).wait()

    inn, out_ = pl.ds(0, T), pl.ds(T, T)

    def send_inner(level):
        k = lax.rem(level, 2)
        return remote(sbuf.at[lax.rem(level, 4), inn], hs.at[k], h_s.at[k], h_r.at[k], sib)

    def send_across(step, p):
        k = lax.rem(step, 2)
        rs = pl.ds(p * T, T)
        return remote(sbuf.at[2 * k, rs], hn.at[k, rs], n_s.at[k, p], n_r.at[k, p], nb)

    def cross(step, p, what):
        @pl.when(joined)
        def _():
            if what == "go":
                send_across(step, p).start()
            else:
                send_across(step, p).wait()

    await_red(0, mbuf)
    relay(0)

    await_red(1, fbuf)
    kinds = lax.broadcasted_iota(I32, (T, 256), 0)
    hot = jnp.where(kinds == mbuf[0:1, :], 1.0, 0.0).astype(F32).T
    embedded = hot[:, 0:1] * table[0:1, :]
    for k in range(1, 4):
        embedded = embedded + hot[:, k : k + 1] * table[k : k + 1, :]
    first = (fbuf[...].astype(F32) + embedded).astype(BF16)
    sbuf[0, pl.ds(pl.multiple_of((1 - c) * T, T), T), :] = first[0:T]
    sbuf[0, pl.ds(pl.multiple_of(c * T, T), T), :] = first[T : 2 * T]

    send_inner(0).start()
    cross(0, 0, "go")
    cross(0, 1, "go")
    relay(1)

    @pl.when(lax.rem(y, 2) == 1)
    def _():
        to_chips(0)

    await_red(2, tbuf)
    trow, tcol = mbuf[1:2, 0:T], mbuf[2:3, 0:T]
    lane = lax.broadcasted_iota(I32, (1, T), 1)
    tlive = jnp.sum(jnp.where(lane == g, mbuf[3:4, 0:T], 0), axis=1, keepdims=True)
    alive = lane < tlive

    def dense(r, cc):
        coef = jnp.where((trow == r) & (tcol == cc) & alive, 1.0, 0.0).astype(F32)
        total = coef[:, 0:1] * tbuf[0].astype(F32)
        for k in range(1, SLOTS):
            total = total + coef[:, k : k + 1] * tbuf[k].astype(F32)
        return total.astype(BF16)

    inner, outer = 2 * t + 1 - c, 2 * t + c
    acat[T : 2 * T, 0:T] = dense(outer, inner)
    acat[T : 2 * T, T : 2 * T] = dense(outer, outer)
    aout[1] = dense(2 * t - 1 + 3 * c, outer)
    aout[0] = dense(2 * t + 2 - 3 * c, inner)
    rim0 = remote(aout.at[0], ain.at[0], a_s.at[0], a_r.at[0], sib)
    rim1 = remote(aout.at[1], ain.at[1], a_s.at[1], a_r.at[1], nb)
    rim2 = remote(acat.at[pl.ds(T, T)], anb, a_s.at[2], a_r.at[2], nb)
    rim0.start()

    @pl.when(joined)
    def _():
        rim1.start()
        rim2.start()

    @pl.when(jnp.logical_not(joined))
    def _():
        ain[1] = jnp.zeros((T, T), BF16)
        anb[...] = jnp.zeros((T, 2 * T), BF16)
        hn[...] = jnp.zeros((2, 2 * T, D), BF16)

    acat[0:T, 0:T] = dense(inner, inner)
    acat[0:T, T : 2 * T] = dense(inner, outer)

    near()
    far()
    own_local.wait()
    rim0.wait()

    @pl.when(joined)
    def _():
        rim1.wait()
        rim2.wait()

    def other_weight(l):
        await_gain(l)
        for q in range(QS):
            await_weight(l, q)

    def update(l, aggregate, before):
        projected = dot(aggregate.astype(BF16), wbuf[l])
        scale = lax.rsqrt(jnp.mean(projected * projected, axis=-1, keepdims=True) + 1e-6)
        normed = projected * scale * gbuf[l][0:1, :]
        return (before.astype(F32) + jax.nn.gelu(normed)).astype(BF16)

    def two_layers(i, carry):
        l = 2 * i
        a, b, n = 2 * lax.rem(i, 2), 2 * lax.rem(i, 2) + 1, lax.rem(2 * i + 2, 4)
        k = lax.rem(i, 2)

        own[...] = dot(acat[...], sbuf[a])

        @pl.when(c == 1)
        def _():
            other_weight(l)

        send_inner(l).wait()
        sbuf[b, inn, :] = update(l, own[inn, :] + dot(ain[0], hs[0]), sbuf[a, inn, :])
        send_inner(l + 1).start()

        cross(i, 0, "take")
        pre[...] = dot(aout[1], sbuf[a, out_, :]) + dot(anb[:, 0:T], hn[k, inn, :])

        @pl.when(c == 0)
        def _():
            other_weight(l + 1)

        cross(i, 1, "take")
        sbuf[b, out_, :] = update(l, own[out_, :] + dot(ain[1], hn[k, out_, :]), sbuf[a, out_, :])
        send_inner(l + 1).wait()
        sbuf[n, inn, :] = update(
            l + 1, dot(acat[inn, :], sbuf[b]) + dot(ain[0], hs[1]), sbuf[b, inn, :]
        )

        @pl.when(i < LAYERS // 2 - 1)
        def _():
            cross(i + 1, 0, "go")
            send_inner(l + 2).start()

        hb[...] = update(
            l, pre[...] + dot(anb[:, T : 2 * T], hn[k, out_, :]), hn[k, out_, :]
        )
        sbuf[n, out_, :] = update(
            l + 1, dot(acat[out_, :], sbuf[b]) + dot(ain[1], hb[...]), sbuf[b, out_, :]
        )

        @pl.when(i < LAYERS // 2 - 1)
        def _():
            cross(i + 1, 1, "go")

        return carry

    lax.fori_loop(0, LAYERS // 2, two_layers, 0)

    last = sbuf[0]
    weight = jnp.broadcast_to(head[...], (8, D))
    top = weight.astype(BF16)
    rest = weight - top.astype(F32)
    mid = rest.astype(BF16)
    low = (rest - mid.astype(F32)).astype(BF16)

    def against(part):
        return lax.dot_general(part, last, (((1,), (1,)), ((), ())), preferred_element_type=F32)

    result = against(top) + against(mid) + against(low)
    obuf[1 - c] = result[:, 0:T]
    obuf[c] = result[:, T : 2 * T]

    @pl.when(moves)
    def _():
        give = remote(obuf, rbuf, o_s, o_r, back)
        give.start()
        give.wait_send()

    @pl.when(stay)
    def _():
        pltpu.make_async_copy(obuf, rbuf, o_r).start()

    for k, dev in enumerate((yp, ym, sib)):
        own_gain(k, dev).wait_send()

    for k, dev in enumerate((yp, ym, sib)):
        for q in range(QS):
            own_weight(k, q, dev).wait_send()

    forward_gain(lm, grel_s.at[0], yp).wait_send()
    for q in (0, 1):
        forward(lm, q, rel_s.at[q], yp).wait_send()
        forward(lp, q + 2, rel_s.at[q + 2], ym).wait_send()
    for l in (lm, lp, l2):
        forward_gain(l, gfw_s.at[l], sib).wait_send()
        for q in range(QS):
            forward(l, q, fw_s.at[l, q], sib).wait_send()

    @pl.when(moves)
    def _():
        for i, (src, dst) in enumerate(red):
            remote(src, dst, red_s.at[i], red_r.at[i], to).wait_send()

    pltpu.make_async_copy(rbuf, rbuf, o_r).wait()
    out[0:1, 0:T] = rbuf[0, 0:1, :]
    out[0:1, T : 2 * T] = rbuf[1, 0:1, :]


def body(features, labels, label_table, tiles, tile_rows, tile_cols, tile_live, weights, gains, head_weight):
    vmem = pl.BlockSpec(memory_space=pltpu.VMEM)
    far = pl.BlockSpec(memory_space=pl.ANY)
    dma = pltpu.SemaphoreType.DMA
    return pl.pallas_call(
        kernel,
        out_shape=jax.ShapeDtypeStruct((1, 2 * T), F32),
        in_specs=[far] * 10,
        out_specs=vmem,
        scratch_shapes=[
            pltpu.VMEM((8, 256), I32),
            pltpu.VMEM((4, D), F32),
            pltpu.VMEM((8, SLOTS), I32),
            pltpu.VMEM((8, SLOTS), I32),
            pltpu.VMEM((1, 8), I32),
            pltpu.VMEM((1, D), BF16),
            pltpu.VMEM((1, D), F32),
            dma((7,)),
            pltpu.VMEM((2 * T, D), BF16),
            pltpu.VMEM((SLOTS, T, T), BF16),
            pltpu.VMEM((8, 256), I32),
            pltpu.VMEM((8, 256), I32),
            pltpu.VMEM((8, D), F32),
            pltpu.VMEM((LAYERS, 8, D), F32),
            pltpu.VMEM((LAYERS, D, D), BF16),
            pltpu.VMEM((4, 2 * T, D), BF16),
            pltpu.VMEM((2, T, D), BF16),
            pltpu.VMEM((2, 2 * T, D), BF16),
            pltpu.VMEM((2 * T, 2 * T), BF16),
            pltpu.VMEM((2, T, T), BF16),
            pltpu.VMEM((2, T, T), BF16),
            pltpu.VMEM((T, 2 * T), BF16),
            pltpu.VMEM((2 * T, D), F32),
            pltpu.VMEM((T, D), F32),
            pltpu.VMEM((T, D), BF16),
            pltpu.VMEM((2, 8, T), F32),
            pltpu.VMEM((2, 8, T), F32),
            dma((3,)),
            dma((3,)),
            dma,
            dma((3, QS)),
            dma((3,)),
            dma((LAYERS, QS)),
            dma((LAYERS,)),
            dma((QS,)),
            dma((1,)),
            dma((LAYERS, QS)),
            dma((LAYERS,)),
            dma((3,)),
            dma((3,)),
            dma((2,)),
            dma((2,)),
            dma((2, 2)),
            dma((2, 2)),
            dma,
            dma,
        ],
        compiler_params=pltpu.CompilerParams(collective_id=0, has_side_effects=True),
    )(
        features, labels, label_table, tiles, tile_rows, tile_cols, tile_live.reshape(1, 8), weights, gains,
        head_weight.reshape(1, D),
    )


def solution(mesh):
    return jax.shard_map(
        body,
        mesh=mesh,
        in_specs=(
            P(None, "shard", None),
            P(None, "shard"),
            P(),
            P(None, "shard", None, None),
            P(None, "shard"),
            P(None, "shard"),
            P(None, "shard"),
            P("section", None, None),
            P("section", None),
            P(),
        ),
        out_specs=P("section", "shard"),
        check_vma=False,
    )
```

```python
import jax
import jax.numpy as jnp
from jax import lax
from jax.experimental import pallas as pl
from jax.experimental.pallas import tpu as pltpu
from jax.sharding import PartitionSpec as P

F32, BF16, I32 = jnp.float32, jnp.bfloat16, jnp.int32
T = 128
D = 512
Q = 128
QS = 4
LAYERS = 8
SLOTS = 6
YN = 4
XN = 4
CHAIN = 32
G1 = 2.0 * (2.0 / 3.141592653589793) ** 0.5
G3 = 4.0 * 0.044715 * G1


def dot(a, b):
    return jnp.dot(a, b, preferred_element_type=F32)


def remote(src, dst, send, recv, dev):
    return pltpu.make_async_remote_copy(
        src_ref=src,
        dst_ref=dst,
        send_sem=send,
        recv_sem=recv,
        device_id=dev,
        device_id_type=pl.DeviceIdType.MESH,
    )


def along(z, hi, f):
    return 2 * hi + jnp.where(lax.rem(z + hi, 2) == 0, f, 1 - f)


def kernel(
    feat, labels_h, table_h, tiles, rows_h, cols_h, live_h, w, gains_h, head_h,
    out,
    labels, table, rows, cols, live, gains, head, in_s,
    fbuf, tbuf, mown, mbuf, gown, gbuf, wbuf, sbuf, hs, hn, acat, aout, ain, anb, own, pre, hb,
    obuf, rbuf,
    red_s, red_r, wloc, os_s, gos_s, w_r, g_r, rel_s, grel_s, fw_s, gfw_s, a_s, a_r, h_s, h_r,
    n_s, n_r, o_s, o_r,
):
    sec = lax.axis_index("section")
    sh = lax.axis_index("shard")
    y, c = lax.div(sec, 2), lax.rem(sec, 2)
    z, x = lax.div(sh, XN), lax.rem(sh, XN)
    hi = lax.div(x, 2)
    xl = lax.rem(x, 2)
    f = jnp.where(lax.rem(z + hi, 2) == 0, xl, 1 - xl)
    g = 2 * y + hi
    t = XN * z + 2 * f + c
    place = 2 * z + f
    sib = (2 * y + 1 - c, sh)
    other = place + 2 * c - 1
    joined = (other >= 0) & (other < CHAIN)
    other = lax.rem(other + CHAIN, CHAIN)
    oz, of = lax.div(other, 2), lax.rem(other, 2)
    nb = (2 * y + 1 - c, XN * oz + along(oz, hi, of))
    up = lax.rem(y + 1, YN)
    down = lax.rem(y + YN - 1, YN)
    opp = lax.rem(y + 2, YN)
    yp = (2 * up + c, sh)
    ym = (2 * down + c, sh)
    to_x = along(z, c, lax.div(x, 2))
    to_sec = 2 * y + lax.rem(x, 2)
    to = (to_sec, XN * z + to_x)
    stay = (to_sec == sec) & (to_x == x)
    back = (g, t)
    moves = jnp.logical_not(stay)

    small = (
        (labels_h, labels), (rows_h, rows), (cols_h, cols), (live_h, live), (gains_h, gains),
        (table_h, table), (head_h, head),
    )
    fetches = [pltpu.make_async_copy(src, dst, in_s.at[i]) for i, (src, dst) in enumerate(small)]
    for fetch in fetches:
        fetch.start()

    barrier = pltpu.get_barrier_semaphore()

    def greet(*devs):
        for dev in devs:
            pl.semaphore_signal(barrier, inc=1, device_id=dev, device_id_type=pl.DeviceIdType.MESH)

    greet(sib, yp, ym)

    @pl.when(joined)
    def _():
        greet(nb)

    @pl.when(moves)
    def _():
        greet(to, back)

    for fetch in fetches:
        fetch.wait()

    mown[...] = jnp.zeros((8, 256), I32)
    mown[0:1, :] = labels[pl.ds(sec, 1), :]
    mown[1:2, 0:SLOTS] = rows[pl.ds(sec, 1), :]
    mown[2:3, 0:SLOTS] = cols[pl.ds(sec, 1), :]
    mown[3:4, 0:8] = live[...]
    gown[...] = jnp.broadcast_to(0.5 * gains[...].astype(F32), (8, D))

    pl.semaphore_wait(barrier, 3 + jnp.where(joined, 1, 0) + jnp.where(moves, 2, 0))

    red = ((mown, mbuf), (feat.at[sec], fbuf), (tiles.at[sec], tbuf))

    @pl.when(moves)
    def _():
        for i, (src, dst) in enumerate(red):
            remote(src, dst, red_s.at[i], red_r.at[i], to).start()

    @pl.when(stay)
    def _():
        for i, (src, dst) in enumerate(red):
            pltpu.make_async_copy(src, dst, red_r.at[i]).start()

    def part(q):
        return pl.ds(q * Q, Q)

    def own_weight(k, q, dev):
        return remote(w.at[0, part(q)], wbuf.at[sec, part(q)], os_s.at[k, q], w_r.at[sec, q], dev)

    def own_gain(k, dev):
        return remote(gown, gbuf.at[sec], gos_s.at[k], g_r.at[sec], dev)

    def forward(l, q, send, dev):
        return remote(wbuf.at[l, part(q)], wbuf.at[l, part(q)], send, w_r.at[l, q], dev)

    def forward_gain(l, send, dev):
        return remote(gbuf.at[l], gbuf.at[l], send, g_r.at[l], dev)

    def await_weight(l, q):
        pltpu.make_async_copy(wbuf.at[l, part(q)], wbuf.at[l, part(q)], w_r.at[l, q]).wait()

    def await_gain(l):
        pltpu.make_async_copy(gbuf.at[l], gbuf.at[l], g_r.at[l]).wait()

    lm, lp, l2 = 2 * down + c, 2 * up + c, 2 * opp + c

    def to_chips(first):
        for q in (0, 1):
            own_weight(0, q + 2 - 2 * first, yp).start()
            own_weight(1, q + 2 * first, ym).start()

    def share(l, q):
        forward(l, q, fw_s.at[l, q], sib).start()

    def share_gain(l):
        forward_gain(l, gfw_s.at[l], sib).start()

    def relay(q):
        if q == 0:
            await_gain(lm)
            forward_gain(lm, grel_s.at[0], yp).start()
            share_gain(lm)
        await_weight(lm, q)
        forward(lm, q, rel_s.at[q], yp).start()
        await_weight(lp, q + 2)
        forward(lp, q + 2, rel_s.at[q + 2], ym).start()
        share(lm, q)
        share(lp, q + 2)

    def service(i):
        l = 2 * i + c

        @pl.when(i == down)
        def _():
            for q in (2, 3):
                await_weight(l, q)
                share(l, q)

        @pl.when(i == up)
        def _():
            await_gain(l)
            share_gain(l)
            for q in (0, 1):
                await_weight(l, q)
                share(l, q)

        @pl.when(i == opp)
        def _():
            await_gain(l)
            share_gain(l)
            for q in (0, 2, 1, 3):
                await_weight(l, q)
                share(l, q)

    own_local = pltpu.make_async_copy(w.at[0], wbuf.at[sec], wloc)
    own_local.start()
    gbuf[sec] = gown[...]

    own_gain(0, yp).start()
    own_gain(1, ym).start()
    to_chips(1)

    @pl.when(lax.rem(y, 2) == 0)
    def _():
        to_chips(0)

    own_gain(2, sib).start()
    for q in range(QS):
        own_weight(2, q, sib).start()

    def await_red(i, dst):
        pltpu.make_async_copy(dst, dst, red_r.at[i]).wait()

    inn, out_ = pl.ds(0, T), pl.ds(T, T)

    def send_inner(level):
        k = lax.rem(level, 2)
        return remote(sbuf.at[lax.rem(level, 4), inn], hs.at[k], h_s.at[k], h_r.at[k], sib)

    def send_across(step, p):
        k = lax.rem(step, 2)
        rs = pl.ds(p * T, T)
        return remote(sbuf.at[2 * k, rs], hn.at[k, rs], n_s.at[k, p], n_r.at[k, p], nb)

    def cross(step, p, what):
        @pl.when(joined)
        def _():
            if what == "go":
                send_across(step, p).start()
            else:
                send_across(step, p).wait()

    await_red(0, mbuf)
    relay(0)

    await_red(1, fbuf)
    kinds = lax.broadcasted_iota(I32, (T, 256), 0)
    hot = jnp.where(kinds == mbuf[0:1, :], 1.0, 0.0).astype(F32).T
    embedded = hot[:, 0:1] * table[0:1, :]
    for k in range(1, 4):
        embedded = embedded + hot[:, k : k + 1] * table[k : k + 1, :]
    first = (fbuf[...].astype(F32) + embedded).astype(BF16)
    sbuf[0, pl.ds(pl.multiple_of((1 - c) * T, T), T), :] = first[0:T]
    sbuf[0, pl.ds(pl.multiple_of(c * T, T), T), :] = first[T : 2 * T]

    send_inner(0).start()
    cross(0, 0, "go")
    cross(0, 1, "go")
    relay(1)

    @pl.when(lax.rem(y, 2) == 1)
    def _():
        to_chips(0)

    await_red(2, tbuf)
    trow, tcol = mbuf[1:2, 0:T], mbuf[2:3, 0:T]
    lane = lax.broadcasted_iota(I32, (1, T), 1)
    tlive = jnp.sum(jnp.where(lane == g, mbuf[3:4, 0:T], 0), axis=1, keepdims=True)
    alive = lane < tlive

    def dense(r, cc):
        coef = jnp.where((trow == r) & (tcol == cc) & alive, 1.0, 0.0).astype(F32)
        total = coef[:, 0:1] * tbuf[0].astype(F32)
        for k in range(1, SLOTS):
            total = total + coef[:, k : k + 1] * tbuf[k].astype(F32)
        return total.astype(BF16)

    inner, outer = 2 * t + 1 - c, 2 * t + c
    acat[T : 2 * T, 0:T] = dense(outer, inner)
    acat[T : 2 * T, T : 2 * T] = dense(outer, outer)
    aout[1] = dense(2 * t - 1 + 3 * c, outer)
    aout[0] = dense(2 * t + 2 - 3 * c, inner)
    rim0 = remote(aout.at[0], ain.at[0], a_s.at[0], a_r.at[0], sib)
    rim1 = remote(aout.at[1], ain.at[1], a_s.at[1], a_r.at[1], nb)
    rim2 = remote(acat.at[pl.ds(T, T)], anb, a_s.at[2], a_r.at[2], nb)
    rim0.start()

    @pl.when(joined)
    def _():
        rim1.start()
        rim2.start()

    @pl.when(jnp.logical_not(joined))
    def _():
        ain[1] = jnp.zeros((T, T), BF16)
        anb[...] = jnp.zeros((T, 2 * T), BF16)
        hn[...] = jnp.zeros((2, 2 * T, D), BF16)

    acat[0:T, 0:T] = dense(inner, inner)
    acat[0:T, T : 2 * T] = dense(inner, outer)

    service(0)
    own_local.wait()
    rim0.wait()

    @pl.when(joined)
    def _():
        rim1.wait()
        rim2.wait()

    def other_weight(l):
        await_gain(l)
        for q in range(QS):
            await_weight(l, q)

    def update(l, aggregate, before):
        projected = dot(aggregate.astype(BF16), wbuf[l])
        scale = lax.rsqrt(jnp.mean(projected * projected, axis=-1, keepdims=True) + 1e-6)
        h = (projected * scale) * gbuf[l][0:1, :]
        gate = jnp.tanh(h * (G1 + G3 * (h * h)))
        return (before.astype(F32) + (h + h * gate)).astype(BF16)

    def two_layers(i, k, final):
        l = 2 * i
        a, b, n = 2 * k, 2 * k + 1, 2 - 2 * k

        def go(p):
            if final is None:
                cross(i + 1, p, "go")
                if p == 0:
                    send_inner(l + 2).start()
            else:
                @pl.when(final)
                def _():
                    cross(i + 1, p, "go")
                    if p == 0:
                        send_inner(l + 2).start()

        def near_outer():
            sbuf[b, out_, :] = update(
                l, own[out_, :] + dot(ain[1], hn[k, out_, :]), sbuf[a, out_, :]
            )

        def far_outer(sl, p):
            hb[...] = update(l, pre[...] + dot(anb[:, sl], hn[k, p, :]), hn[k, out_, :])

        def next_inner():
            sbuf[n, inn, :] = update(
                l + 1, dot(acat[inn, :], sbuf[b]) + dot(ain[0], hs[1]), sbuf[b, inn, :]
            )
            go(0)

        def next_outer():
            sbuf[n, out_, :] = update(
                l + 1, dot(acat[out_, :], sbuf[b]) + dot(ain[1], hb[...]), sbuf[b, out_, :]
            )
            go(1)

        own[...] = dot(acat[...], sbuf[a])

        @pl.when(c == 1)
        def _():
            other_weight(l)

        send_inner(l).wait()
        sbuf[b, inn, :] = update(l, own[inn, :] + dot(ain[0], hs[0]), sbuf[a, inn, :])
        send_inner(l + 1).start()

        @pl.when(c == 0)
        def _():
            other_weight(l + 1)

        left, right = slice(0, T), slice(T, 2 * T)
        if k == 0:
            cross(i, 0, "take")
            pre[...] = dot(aout[1], sbuf[a, out_, :]) + dot(anb[:, left], hn[k, inn, :])
            cross(i, 1, "take")
            near_outer()
            far_outer(right, out_)
            next_outer()
            send_inner(l + 1).wait()
            next_inner()
        else:
            cross(i, 1, "take")
            near_outer()
            send_inner(l + 1).wait()
            next_inner()
            pre[...] = dot(aout[1], sbuf[a, out_, :]) + dot(anb[:, right], hn[k, out_, :])
            cross(i, 0, "take")
            far_outer(left, inn)
            next_outer()

    def four_layers(j, carry):
        two_layers(2 * j, 0, None)
        service(2 * j + 1)
        two_layers(2 * j + 1, 1, j < LAYERS // 4 - 1)

        @pl.when(j < LAYERS // 4 - 1)
        def _():
            service(2 * j + 2)

        return carry

    lax.fori_loop(0, LAYERS // 4, four_layers, 0)

    last = sbuf[0]
    weight = jnp.broadcast_to(head[...], (8, D))
    top = weight.astype(BF16)
    rest = weight - top.astype(F32)
    mid = rest.astype(BF16)
    low = (rest - mid.astype(F32)).astype(BF16)

    def against(part):
        return lax.dot_general(part, last, (((1,), (1,)), ((), ())), preferred_element_type=F32)

    result = against(top) + against(mid) + against(low)
    obuf[1 - c] = result[:, 0:T]
    obuf[c] = result[:, T : 2 * T]

    @pl.when(moves)
    def _():
        give = remote(obuf, rbuf, o_s, o_r, back)
        give.start()
        give.wait_send()

    @pl.when(stay)
    def _():
        pltpu.make_async_copy(obuf, rbuf, o_r).start()

    for k, dev in enumerate((yp, ym, sib)):
        own_gain(k, dev).wait_send()

    for k, dev in enumerate((yp, ym, sib)):
        for q in range(QS):
            own_weight(k, q, dev).wait_send()

    forward_gain(lm, grel_s.at[0], yp).wait_send()
    for q in (0, 1):
        forward(lm, q, rel_s.at[q], yp).wait_send()
        forward(lp, q + 2, rel_s.at[q + 2], ym).wait_send()
    for l in (lm, lp, l2):
        forward_gain(l, gfw_s.at[l], sib).wait_send()
        for q in range(QS):
            forward(l, q, fw_s.at[l, q], sib).wait_send()

    @pl.when(moves)
    def _():
        for i, (src, dst) in enumerate(red):
            remote(src, dst, red_s.at[i], red_r.at[i], to).wait_send()

    pltpu.make_async_copy(rbuf, rbuf, o_r).wait()
    out[0:1, 0:T] = rbuf[0, 0:1, :]
    out[0:1, T : 2 * T] = rbuf[1, 0:1, :]


def body(features, labels, label_table, tiles, tile_rows, tile_cols, tile_live, weights, gains, head_weight):
    vmem = pl.BlockSpec(memory_space=pltpu.VMEM)
    far = pl.BlockSpec(memory_space=pl.ANY)
    dma = pltpu.SemaphoreType.DMA
    return pl.pallas_call(
        kernel,
        out_shape=jax.ShapeDtypeStruct((1, 2 * T), F32),
        in_specs=[far] * 10,
        out_specs=vmem,
        scratch_shapes=[
            pltpu.VMEM((8, 256), I32),
            pltpu.VMEM((4, D), F32),
            pltpu.VMEM((8, SLOTS), I32),
            pltpu.VMEM((8, SLOTS), I32),
            pltpu.VMEM((1, 8), I32),
            pltpu.VMEM((1, D), BF16),
            pltpu.VMEM((1, D), F32),
            dma((7,)),
            pltpu.VMEM((2 * T, D), BF16),
            pltpu.VMEM((SLOTS, T, T), BF16),
            pltpu.VMEM((8, 256), I32),
            pltpu.VMEM((8, 256), I32),
            pltpu.VMEM((8, D), F32),
            pltpu.VMEM((LAYERS, 8, D), F32),
            pltpu.VMEM((LAYERS, D, D), BF16),
            pltpu.VMEM((4, 2 * T, D), BF16),
            pltpu.VMEM((2, T, D), BF16),
            pltpu.VMEM((2, 2 * T, D), BF16),
            pltpu.VMEM((2 * T, 2 * T), BF16),
            pltpu.VMEM((2, T, T), BF16),
            pltpu.VMEM((2, T, T), BF16),
            pltpu.VMEM((T, 2 * T), BF16),
            pltpu.VMEM((2 * T, D), F32),
            pltpu.VMEM((T, D), F32),
            pltpu.VMEM((T, D), BF16),
            pltpu.VMEM((2, 8, T), F32),
            pltpu.VMEM((2, 8, T), F32),
            dma((3,)),
            dma((3,)),
            dma,
            dma((3, QS)),
            dma((3,)),
            dma((LAYERS, QS)),
            dma((LAYERS,)),
            dma((QS,)),
            dma((1,)),
            dma((LAYERS, QS)),
            dma((LAYERS,)),
            dma((3,)),
            dma((3,)),
            dma((2,)),
            dma((2,)),
            dma((2, 2)),
            dma((2, 2)),
            dma,
            dma,
        ],
        compiler_params=pltpu.CompilerParams(collective_id=0, has_side_effects=True),
    )(
        features, labels, label_table, tiles, tile_rows, tile_cols, tile_live.reshape(1, 8), weights, gains,
        head_weight.reshape(1, D),
    )


def solution(mesh):
    return jax.shard_map(
        body,
        mesh=mesh,
        in_specs=(
            P(None, "shard", None),
            P(None, "shard"),
            P(),
            P(None, "shard", None, None),
            P(None, "shard"),
            P(None, "shard"),
            P(None, "shard"),
            P("section", None, None),
            P("section", None),
            P(),
        ),
        out_specs=P("section", "shard"),
        check_vma=False,
    )
```

```python
import jax
import jax.numpy as jnp
from jax import lax
from jax.experimental import pallas as pl
from jax.experimental.pallas import tpu as pltpu
from jax.sharding import PartitionSpec as P

F32, BF16, I32 = jnp.float32, jnp.bfloat16, jnp.int32
T = 128
D = 512
Q = 128
QS = 4
LAYERS = 8
SLOTS = 6
YN = 4
XN = 4
CHAIN = 32
G1 = 2.0 * (2.0 / 3.141592653589793) ** 0.5
G3 = 4.0 * 0.044715 * G1


def dot(a, b):
    return jnp.dot(a, b, preferred_element_type=F32)


def remote(src, dst, send, recv, dev):
    return pltpu.make_async_remote_copy(
        src_ref=src,
        dst_ref=dst,
        send_sem=send,
        recv_sem=recv,
        device_id=dev,
        device_id_type=pl.DeviceIdType.MESH,
    )


def split(dev):
    sec, sh = dev
    return lax.div(sec, 2), lax.rem(sec, 2), lax.div(sh, XN), lax.rem(sh, XN)


def along(z, hi, f):
    return 2 * hi + jnp.where(lax.rem(z + hi, 2) == 0, f, 1 - f)


def work_of(dev):
    y, c, z, x = split(dev)
    hi, xl = lax.div(x, 2), lax.rem(x, 2)
    f = jnp.where(lax.rem(z + hi, 2) == 0, xl, 1 - xl)
    return 2 * y + hi, XN * z + 2 * f + c


def worker(dev):
    y, c, z, x = split(dev)
    return 2 * y + lax.rem(x, 2), XN * z + along(z, c, lax.div(x, 2))


def other_core(dev):
    y, c, z, x = split(dev)
    return 2 * y + 1 - c, dev[1]


def across(dev):
    y, c, z, x = split(dev)
    hi = lax.div(x, 2)
    place = lax.div(work_of(dev)[1], 2) + 2 * c - 1
    joined = (place >= 0) & (place < CHAIN)
    place = lax.rem(place + CHAIN, CHAIN)
    oz, of = lax.div(place, 2), lax.rem(place, 2)
    return (2 * y + 1 - c, XN * oz + along(oz, hi, of)), joined


def same(p, q):
    return (p[0] == q[0]) & (p[1] == q[1])


def kernel(
    feat, labels_h, table_h, tiles, rows_h, cols_h, live_h, w, gains_h, head_h,
    out,
    labels, table, rows, cols, live, gains, head, in_s,
    fbuf, tbuf, mown, mbuf, gown, gbuf, wbuf, sbuf, hs, hn, acat, pk, fk, rk, opk, npk, ain,
    emb, own, pre, hb,
    obuf, rbuf,
    red_s, red_r, wloc, os_s, gos_s, w_r, g_r, rel_s, grel_s, fw_s, gfw_s, t_s, h_s, h_r,
    n_s, n_r, o_s, o_r,
):
    sec = lax.axis_index("section")
    sh = lax.axis_index("shard")
    me = (sec, sh)
    y, c, z, x = split(me)
    sib = other_core(me)
    nb, joined = across(me)
    up = lax.rem(y + 1, YN)
    down = lax.rem(y + YN - 1, YN)
    opp = lax.rem(y + 2, YN)
    yp = (2 * up + c, sh)
    ym = (2 * down + c, sh)
    to = worker(me)
    to_sib = other_core(to)
    to_nb, to_joined = across(to)
    back, back_sib, back_nb = work_of(me), work_of(sib), work_of(nb)
    moves = jnp.logical_not(same(to, me))
    stay = same(to, me)
    rim_moves = jnp.logical_not(same(to_sib, me))
    far_moves = to_joined & jnp.logical_not(same(to_nb, me))
    far_stays = to_joined & same(to_nb, me)
    far_comes = joined & jnp.logical_not(same(back_nb, me))

    small = (
        (labels_h, labels), (rows_h, rows), (cols_h, cols), (live_h, live), (gains_h, gains),
        (table_h, table), (head_h, head),
    )
    fetches = [pltpu.make_async_copy(src, dst, in_s.at[i]) for i, (src, dst) in enumerate(small)]
    for fetch in fetches:
        fetch.start()
    get_tiles = pltpu.make_async_copy(tiles.at[sec], tbuf, t_s)
    get_tiles.start()

    barrier = pltpu.get_barrier_semaphore()

    def greet(*devs):
        for dev in devs:
            pl.semaphore_signal(barrier, inc=1, device_id=dev, device_id_type=pl.DeviceIdType.MESH)

    greet(sib, yp, ym)

    @pl.when(joined)
    def _():
        greet(nb)

    @pl.when(moves)
    def _():
        greet(to, back)

    @pl.when(rim_moves)
    def _():
        greet(to_sib, back_sib)

    @pl.when(far_moves)
    def _():
        greet(to_nb)

    @pl.when(far_comes)
    def _():
        greet(back_nb)

    for fetch in fetches:
        fetch.wait()

    mown[...] = jnp.broadcast_to(labels[pl.ds(sec, 1), :], (8, 256))
    gown[...] = jnp.broadcast_to(0.5 * gains[...].astype(F32), (8, D))
    trow, tcol = rows[pl.ds(sec, 1), :], cols[pl.ds(sec, 1), :]
    lane = lax.broadcasted_iota(I32, (1, 8), 1)
    tlive = jnp.sum(jnp.where(lane == sec, live[...], 0), axis=1, keepdims=True)
    alive = lax.broadcasted_iota(I32, (1, SLOTS), 1) < tlive
    get_tiles.wait()

    def dense(r, cc):
        coef = jnp.where((trow == r) & (tcol == cc) & alive, 1.0, 0.0).astype(F32)
        total = coef[:, 0:1] * tbuf[0].astype(F32)
        for k in range(1, SLOTS):
            total = total + coef[:, k : k + 1] * tbuf[k].astype(F32)
        return total.astype(BF16)

    tc = lax.rem(x, 2)
    inner, outer = 2 * sh + 1 - tc, 2 * sh + tc
    pk[:, 0:T] = dense(outer, inner)
    pk[:, T : 2 * T] = dense(outer, outer)
    pk[:, 2 * T : 3 * T] = dense(2 * sh - 1 + 3 * tc, outer)
    fk[:, 0:T] = dense(inner, inner)
    fk[:, T : 2 * T] = dense(inner, outer)
    rk[...] = dense(2 * sh + 2 - 3 * tc, inner)

    amount = jnp.where(moves, 2, 0) + jnp.where(rim_moves, 2, 0) + jnp.where(far_moves, 1, 0)
    amount = amount + jnp.where(far_comes, 1, 0) + jnp.where(joined, 1, 0)
    pl.semaphore_wait(barrier, 3 + amount)

    fo, fi = pl.ds(pl.multiple_of(tc * T, T), T), pl.ds(pl.multiple_of((1 - tc) * T, T), T)
    red = (
        (mown, mbuf), (feat.at[sec, fo], fbuf.at[fo]), (feat.at[sec, fi], fbuf.at[fi]),
        (pk, opk), (fk, acat.at[pl.ds(0, T)]),
    )
    NPK, RIM = 5, 6

    @pl.when(moves)
    def _():
        for i, (src, dst) in enumerate(red):
            remote(src, dst, red_s.at[i], red_r.at[i], to).start()

    @pl.when(stay)
    def _():
        for i, (src, dst) in enumerate(red):
            pltpu.make_async_copy(src, dst, red_r.at[i]).start()

    give_far = remote(pk, npk, red_s.at[NPK], red_r.at[NPK], to_nb)
    give_rim = remote(rk, ain, red_s.at[RIM], red_r.at[RIM], to_sib)

    @pl.when(far_moves)
    def _():
        give_far.start()

    @pl.when(far_stays)
    def _():
        pltpu.make_async_copy(pk, npk, red_r.at[NPK]).start()

    @pl.when(rim_moves)
    def _():
        give_rim.start()

    @pl.when(jnp.logical_not(rim_moves))
    def _():
        pltpu.make_async_copy(rk, ain, red_r.at[RIM]).start()

    def part(q):
        return pl.ds(q * Q, Q)

    def own_weight(k, q, dev):
        return remote(w.at[0, part(q)], wbuf.at[sec, part(q)], os_s.at[k, q], w_r.at[sec, q], dev)

    def own_gain(k, dev):
        return remote(gown, gbuf.at[sec], gos_s.at[k], g_r.at[sec], dev)

    def forward(l, q, send, dev):
        return remote(wbuf.at[l, part(q)], wbuf.at[l, part(q)], send, w_r.at[l, q], dev)

    def forward_gain(l, send, dev):
        return remote(gbuf.at[l], gbuf.at[l], send, g_r.at[l], dev)

    def await_weight(l, q):
        pltpu.make_async_copy(wbuf.at[l, part(q)], wbuf.at[l, part(q)], w_r.at[l, q]).wait()

    def await_gain(l):
        pltpu.make_async_copy(gbuf.at[l], gbuf.at[l], g_r.at[l]).wait()

    lm, lp, l2 = 2 * down + c, 2 * up + c, 2 * opp + c

    def to_chips(first):
        for q in (0, 1):
            own_weight(0, q + 2 - 2 * first, yp).start()
            own_weight(1, q + 2 * first, ym).start()

    def share(l, q):
        forward(l, q, fw_s.at[l, q], sib).start()

    def share_gain(l):
        forward_gain(l, gfw_s.at[l], sib).start()

    def relay(q):
        if q == 0:
            await_gain(lm)
            forward_gain(lm, grel_s.at[0], yp).start()
            share_gain(lm)
        await_weight(lm, q)
        forward(lm, q, rel_s.at[q], yp).start()
        await_weight(lp, q + 2)
        forward(lp, q + 2, rel_s.at[q + 2], ym).start()
        share(lm, q)
        share(lp, q + 2)

    def service(i):
        l = 2 * i + c

        @pl.when(i == down)
        def _():
            for q in (2, 3):
                await_weight(l, q)
                share(l, q)

        @pl.when(i == up)
        def _():
            await_gain(l)
            share_gain(l)
            for q in (0, 1):
                await_weight(l, q)
                share(l, q)

        @pl.when(i == opp)
        def _():
            await_gain(l)
            share_gain(l)
            for q in (0, 2, 1, 3):
                await_weight(l, q)
                share(l, q)

    own_local = pltpu.make_async_copy(w.at[0], wbuf.at[sec], wloc)
    own_local.start()
    gbuf[sec] = gown[...]

    own_gain(0, yp).start()
    own_gain(1, ym).start()
    to_chips(1)

    @pl.when(lax.rem(y, 2) == 0)
    def _():
        to_chips(0)

    own_gain(2, sib).start()
    for q in range(QS):
        own_weight(2, q, sib).start()

    def await_red(i, dst):
        pltpu.make_async_copy(dst, dst, red_r.at[i]).wait()

    @pl.when(jnp.logical_not(joined))
    def _():
        npk[...] = jnp.zeros((T, 3 * T), BF16)
        hn[...] = jnp.zeros((2, 2 * T, D), BF16)

    inn, out_ = pl.ds(0, T), pl.ds(T, T)

    def send_inner(level):
        k = lax.rem(level, 2)
        return remote(sbuf.at[lax.rem(level, 4), inn], hs.at[k], h_s.at[k], h_r.at[k], sib)

    def send_across(step, p):
        k = lax.rem(step, 2)
        rs = pl.ds(p * T, T)
        return remote(sbuf.at[2 * k, rs], hn.at[k, rs], n_s.at[k, p], n_r.at[k, p], nb)

    def cross(step, p, what):
        @pl.when(joined)
        def _():
            if what == "go":
                send_across(step, p).start()
            else:
                send_across(step, p).wait()

    await_red(0, mbuf)
    kinds = lax.broadcasted_iota(I32, (T, 256), 0)
    hot = jnp.where(kinds == mbuf[0:1, :], 1.0, 0.0).astype(F32).T
    embedded = hot[:, 0:1] * table[0:1, :]
    for k in range(1, 4):
        embedded = embedded + hot[:, k : k + 1] * table[k : k + 1, :]
    emb[...] = embedded

    ro, ri = pl.ds(pl.multiple_of(c * T, T), T), pl.ds(pl.multiple_of((1 - c) * T, T), T)
    await_red(1, fbuf.at[ro])
    sbuf[0, out_, :] = (fbuf[ro, :].astype(F32) + emb[ro, :]).astype(BF16)
    cross(0, 1, "go")
    relay(0)
    await_red(2, fbuf.at[ri])
    sbuf[0, inn, :] = (fbuf[ri, :].astype(F32) + emb[ri, :]).astype(BF16)
    cross(0, 0, "go")
    send_inner(0).start()
    relay(1)

    @pl.when(lax.rem(y, 2) == 1)
    def _():
        to_chips(0)

    await_red(3, opk)
    await_red(4, acat.at[pl.ds(0, T)])
    acat[T : 2 * T, :] = opk[:, 0 : 2 * T]
    service(0)
    own_local.wait()
    await_red(RIM, ain)

    @pl.when(joined)
    def _():
        await_red(NPK, npk)

    def other_weight(l):
        await_gain(l)
        for q in range(QS):
            await_weight(l, q)

    def update(l, aggregate, before):
        projected = dot(aggregate.astype(BF16), wbuf[l])
        scale = lax.rsqrt(jnp.mean(projected * projected, axis=-1, keepdims=True) + 1e-6)
        h = (projected * scale) * gbuf[l][0:1, :]
        gate = jnp.tanh(h * (G1 + G3 * (h * h)))
        return (before.astype(F32) + (h + h * gate)).astype(BF16)

    def two_layers(i, k, final):
        l = 2 * i
        a, b, n = 2 * k, 2 * k + 1, 2 - 2 * k

        def go(p):
            if final is None:
                cross(i + 1, p, "go")
                if p == 0:
                    send_inner(l + 2).start()
            else:
                @pl.when(final)
                def _():
                    cross(i + 1, p, "go")
                    if p == 0:
                        send_inner(l + 2).start()

        def near_outer():
            sbuf[b, out_, :] = update(
                l, own[out_, :] + dot(npk[:, 2 * T : 3 * T], hn[k, out_, :]), sbuf[a, out_, :]
            )

        def far_outer(sl, p):
            hb[...] = update(l, pre[...] + dot(npk[:, sl], hn[k, p, :]), hn[k, out_, :])

        def next_inner():
            sbuf[n, inn, :] = update(
                l + 1, dot(acat[inn, :], sbuf[b]) + dot(ain[...], hs[1]), sbuf[b, inn, :]
            )
            go(0)

        def next_outer():
            sbuf[n, out_, :] = update(
                l + 1, dot(acat[out_, :], sbuf[b]) + dot(npk[:, 2 * T : 3 * T], hb[...]), sbuf[b, out_, :]
            )
            go(1)

        own[...] = dot(acat[...], sbuf[a])

        @pl.when(c == 1)
        def _():
            other_weight(l)

        send_inner(l).wait()
        sbuf[b, inn, :] = update(l, own[inn, :] + dot(ain[...], hs[0]), sbuf[a, inn, :])
        send_inner(l + 1).start()

        @pl.when(c == 0)
        def _():
            other_weight(l + 1)

        left, right = slice(0, T), slice(T, 2 * T)
        if k == 1:
            cross(i, 0, "take")
            pre[...] = dot(opk[:, 2 * T : 3 * T], sbuf[a, out_, :]) + dot(npk[:, left], hn[k, inn, :])
            cross(i, 1, "take")
            near_outer()
            far_outer(right, out_)
            next_outer()
            send_inner(l + 1).wait()
            next_inner()
        else:
            cross(i, 1, "take")
            near_outer()
            send_inner(l + 1).wait()
            next_inner()
            pre[...] = dot(opk[:, 2 * T : 3 * T], sbuf[a, out_, :]) + dot(npk[:, right], hn[k, out_, :])
            cross(i, 0, "take")
            far_outer(left, inn)
            next_outer()

    def four_layers(j, carry):
        two_layers(2 * j, 0, None)
        service(2 * j + 1)
        two_layers(2 * j + 1, 1, j < LAYERS // 4 - 1)

        @pl.when(j < LAYERS // 4 - 1)
        def _():
            service(2 * j + 2)

        return carry

    lax.fori_loop(0, LAYERS // 4, four_layers, 0)

    last = sbuf[0]
    weight = jnp.broadcast_to(head[...], (8, D))
    top = weight.astype(BF16)
    rest = weight - top.astype(F32)
    mid = rest.astype(BF16)
    low = (rest - mid.astype(F32)).astype(BF16)

    def against(part):
        return lax.dot_general(part, last, (((1,), (1,)), ((), ())), preferred_element_type=F32)

    result = against(top) + against(mid) + against(low)
    obuf[1 - c] = result[:, 0:T]
    obuf[c] = result[:, T : 2 * T]

    @pl.when(moves)
    def _():
        give = remote(obuf, rbuf, o_s, o_r, back)
        give.start()
        give.wait_send()

    @pl.when(stay)
    def _():
        pltpu.make_async_copy(obuf, rbuf, o_r).start()

    for k, dev in enumerate((yp, ym, sib)):
        own_gain(k, dev).wait_send()

    for k, dev in enumerate((yp, ym, sib)):
        for q in range(QS):
            own_weight(k, q, dev).wait_send()

    forward_gain(lm, grel_s.at[0], yp).wait_send()
    for q in (0, 1):
        forward(lm, q, rel_s.at[q], yp).wait_send()
        forward(lp, q + 2, rel_s.at[q + 2], ym).wait_send()
    for l in (lm, lp, l2):
        forward_gain(l, gfw_s.at[l], sib).wait_send()
        for q in range(QS):
            forward(l, q, fw_s.at[l, q], sib).wait_send()

    @pl.when(moves)
    def _():
        for i, (src, dst) in enumerate(red):
            remote(src, dst, red_s.at[i], red_r.at[i], to).wait_send()

    @pl.when(far_moves)
    def _():
        give_far.wait_send()

    @pl.when(rim_moves)
    def _():
        give_rim.wait_send()

    pltpu.make_async_copy(rbuf, rbuf, o_r).wait()
    out[0:1, 0:T] = rbuf[0, 0:1, :]
    out[0:1, T : 2 * T] = rbuf[1, 0:1, :]


def body(features, labels, label_table, tiles, tile_rows, tile_cols, tile_live, weights, gains, head_weight):
    vmem = pl.BlockSpec(memory_space=pltpu.VMEM)
    far = pl.BlockSpec(memory_space=pl.ANY)
    dma = pltpu.SemaphoreType.DMA
    return pl.pallas_call(
        kernel,
        out_shape=jax.ShapeDtypeStruct((1, 2 * T), F32),
        in_specs=[far] * 10,
        out_specs=vmem,
        scratch_shapes=[
            pltpu.VMEM((8, 256), I32),
            pltpu.VMEM((4, D), F32),
            pltpu.VMEM((8, SLOTS), I32),
            pltpu.VMEM((8, SLOTS), I32),
            pltpu.VMEM((1, 8), I32),
            pltpu.VMEM((1, D), BF16),
            pltpu.VMEM((1, D), F32),
            dma((7,)),
            pltpu.VMEM((2 * T, D), BF16),
            pltpu.VMEM((SLOTS, T, T), BF16),
            pltpu.VMEM((8, 256), I32),
            pltpu.VMEM((8, 256), I32),
            pltpu.VMEM((8, D), F32),
            pltpu.VMEM((LAYERS, 8, D), F32),
            pltpu.VMEM((LAYERS, D, D), BF16),
            pltpu.VMEM((4, 2 * T, D), BF16),
            pltpu.VMEM((2, T, D), BF16),
            pltpu.VMEM((2, 2 * T, D), BF16),
            pltpu.VMEM((2 * T, 2 * T), BF16),
            pltpu.VMEM((T, 3 * T), BF16),
            pltpu.VMEM((T, 2 * T), BF16),
            pltpu.VMEM((T, T), BF16),
            pltpu.VMEM((T, 3 * T), BF16),
            pltpu.VMEM((T, 3 * T), BF16),
            pltpu.VMEM((T, T), BF16),
            pltpu.VMEM((2 * T, D), F32),
            pltpu.VMEM((2 * T, D), F32),
            pltpu.VMEM((T, D), F32),
            pltpu.VMEM((T, D), BF16),
            pltpu.VMEM((2, 8, T), F32),
            pltpu.VMEM((2, 8, T), F32),
            dma((7,)),
            dma((7,)),
            dma,
            dma((3, QS)),
            dma((3,)),
            dma((LAYERS, QS)),
            dma((LAYERS,)),
            dma((QS,)),
            dma((1,)),
            dma((LAYERS, QS)),
            dma((LAYERS,)),
            dma,
            dma((2,)),
            dma((2,)),
            dma((2, 2)),
            dma((2, 2)),
            dma,
            dma,
        ],
        compiler_params=pltpu.CompilerParams(collective_id=0, has_side_effects=True),
    )(
        features, labels, label_table, tiles, tile_rows, tile_cols, tile_live.reshape(1, 8), weights, gains,
        head_weight.reshape(1, D),
    )


def solution(mesh):
    return jax.shard_map(
        body,
        mesh=mesh,
        in_specs=(
            P(None, "shard", None),
            P(None, "shard"),
            P(),
            P(None, "shard", None, None),
            P(None, "shard"),
            P(None, "shard"),
            P(None, "shard"),
            P("section", None, None),
            P("section", None),
            P(),
        ),
        out_specs=P("section", "shard"),
        check_vma=False,
    )
```

```python
import jax
import jax.numpy as jnp
from jax import lax
from jax.experimental import pallas as pl
from jax.experimental.pallas import tpu as pltpu
from jax.sharding import PartitionSpec as P

F32, BF16, I32 = jnp.float32, jnp.bfloat16, jnp.int32
T = 128
D = 512
Q = 128
QS = 4
LAYERS = 8
SLOTS = 6
YN = 4
XN = 4
CHAIN = 32
G1 = 2.0 * (2.0 / 3.141592653589793) ** 0.5
G3 = 4.0 * 0.044715 * G1


def dot(a, b):
    return jnp.dot(a, b, preferred_element_type=F32)


def remote(src, dst, send, recv, dev):
    return pltpu.make_async_remote_copy(
        src_ref=src,
        dst_ref=dst,
        send_sem=send,
        recv_sem=recv,
        device_id=dev,
        device_id_type=pl.DeviceIdType.MESH,
    )


def split(dev):
    sec, sh = dev
    return lax.div(sec, 2), lax.rem(sec, 2), lax.div(sh, XN), lax.rem(sh, XN)


def along(z, hi, f):
    return 2 * hi + jnp.where(lax.rem(z + hi, 2) == 0, f, 1 - f)


def work_of(dev):
    y, c, z, x = split(dev)
    hi, xl = lax.div(x, 2), lax.rem(x, 2)
    f = jnp.where(lax.rem(z + hi, 2) == 0, xl, 1 - xl)
    return 2 * y + hi, XN * z + 2 * f + c


def worker(dev):
    y, c, z, x = split(dev)
    return 2 * y + lax.rem(x, 2), XN * z + along(z, c, lax.div(x, 2))


def other_core(dev):
    y, c, z, x = split(dev)
    return 2 * y + 1 - c, dev[1]


def across(dev):
    y, c, z, x = split(dev)
    hi = lax.div(x, 2)
    place = lax.div(work_of(dev)[1], 2) + 2 * c - 1
    joined = (place >= 0) & (place < CHAIN)
    place = lax.rem(place + CHAIN, CHAIN)
    oz, of = lax.div(place, 2), lax.rem(place, 2)
    return (2 * y + 1 - c, XN * oz + along(oz, hi, of)), joined


def same(p, q):
    return (p[0] == q[0]) & (p[1] == q[1])


def kernel(
    feat, labels_h, table_h, tiles, rows_h, cols_h, live_h, w, gains_h, head_h,
    out,
    labels, table, rows, cols, live, gains, head, in_s,
    fbuf, tbuf, mown, mbuf, gown, gbuf, wbuf, sbuf, hs, hn, acat, pk, fk, rk, opk, npk, ain,
    emb, own, pre, hb,
    obuf, rbuf,
    red_s, red_r, wloc, os_s, gos_s, w_r, g_r, rel_s, grel_s, fw_s, gfw_s, t_s, h_s, h_r,
    n_s, n_r, o_s, o_r,
):
    sec = lax.axis_index("section")
    sh = lax.axis_index("shard")
    me = (sec, sh)
    y, c, z, x = split(me)
    sib = other_core(me)
    nb, joined = across(me)
    up = lax.rem(y + 1, YN)
    down = lax.rem(y + YN - 1, YN)
    opp = lax.rem(y + 2, YN)
    yp = (2 * up + c, sh)
    ym = (2 * down + c, sh)
    to = worker(me)
    to_sib = other_core(to)
    to_nb, to_joined = across(to)
    back, back_sib, back_nb = work_of(me), work_of(sib), work_of(nb)
    moves = jnp.logical_not(same(to, me))
    stay = same(to, me)
    rim_moves = jnp.logical_not(same(to_sib, me))
    far_moves = to_joined & jnp.logical_not(same(to_nb, me))
    far_stays = to_joined & same(to_nb, me)
    far_comes = joined & jnp.logical_not(same(back_nb, me))

    small = (
        (labels_h, labels), (rows_h, rows), (cols_h, cols), (live_h, live), (gains_h, gains),
        (table_h, table), (head_h, head),
    )
    fetches = [pltpu.make_async_copy(src, dst, in_s.at[i]) for i, (src, dst) in enumerate(small)]
    for fetch in fetches:
        fetch.start()
    get_tiles = pltpu.make_async_copy(tiles.at[sec], tbuf, t_s)
    get_tiles.start()

    barrier = pltpu.get_barrier_semaphore()

    def greet(*devs):
        for dev in devs:
            pl.semaphore_signal(barrier, inc=1, device_id=dev, device_id_type=pl.DeviceIdType.MESH)

    greet(sib, yp, ym)

    @pl.when(joined)
    def _():
        greet(nb)

    @pl.when(moves)
    def _():
        greet(to, back)

    @pl.when(rim_moves)
    def _():
        greet(to_sib, back_sib)

    @pl.when(far_moves)
    def _():
        greet(to_nb)

    @pl.when(far_comes)
    def _():
        greet(back_nb)

    for fetch in fetches:
        fetch.wait()

    mown[...] = jnp.broadcast_to(labels[pl.ds(sec, 1), :], (8, 256))
    gown[...] = jnp.broadcast_to(0.5 * gains[...].astype(F32), (8, D))
    amount = jnp.where(moves, 2, 0) + jnp.where(rim_moves, 2, 0) + jnp.where(far_moves, 1, 0)
    amount = amount + jnp.where(far_comes, 1, 0) + jnp.where(joined, 1, 0)
    pl.semaphore_wait(barrier, 3 + amount)

    tc = lax.rem(x, 2)
    fo, fi = pl.ds(pl.multiple_of(tc * T, T), T), pl.ds(pl.multiple_of((1 - tc) * T, T), T)
    red = (
        (mown, mbuf), (feat.at[sec, fo], fbuf.at[fo]), (feat.at[sec, fi], fbuf.at[fi]),
        (pk, opk), (fk, acat.at[pl.ds(0, T)]),
    )
    def part(q):
        return pl.ds(q * Q, Q)

    def own_weight(k, q, dev):
        return remote(w.at[0, part(q)], wbuf.at[sec, part(q)], os_s.at[k, q], w_r.at[sec, q], dev)

    def own_gain(k, dev):
        return remote(gown, gbuf.at[sec], gos_s.at[k], g_r.at[sec], dev)

    def forward(l, q, send, dev):
        return remote(wbuf.at[l, part(q)], wbuf.at[l, part(q)], send, w_r.at[l, q], dev)

    def forward_gain(l, send, dev):
        return remote(gbuf.at[l], gbuf.at[l], send, g_r.at[l], dev)

    def await_weight(l, q):
        pltpu.make_async_copy(wbuf.at[l, part(q)], wbuf.at[l, part(q)], w_r.at[l, q]).wait()

    def await_gain(l):
        pltpu.make_async_copy(gbuf.at[l], gbuf.at[l], g_r.at[l]).wait()

    lm, lp, l2 = 2 * down + c, 2 * up + c, 2 * opp + c

    def send_up(q):
        for k in (q, q + 1):
            own_weight(0, k, yp).start()

    def send_down(q):
        for k in (q, q + 1):
            own_weight(1, k, ym).start()

    def share(l, q):
        forward(l, q, fw_s.at[l, q], sib).start()

    def share_gain(l):
        forward_gain(l, gfw_s.at[l], sib).start()

    def relay(q):
        if q == 0:
            await_gain(lm)
            forward_gain(lm, grel_s.at[0], yp).start()
            share_gain(lm)
        await_weight(lm, q)
        forward(lm, q, rel_s.at[q], yp).start()
        await_weight(lp, q + 2)
        forward(lp, q + 2, rel_s.at[q + 2], ym).start()
        share(lm, q)
        share(lp, q + 2)

    def service(i):
        l = 2 * i + c

        @pl.when(i == down)
        def _():
            for q in (2, 3):
                await_weight(l, q)
                share(l, q)

        @pl.when(i == up)
        def _():
            await_gain(l)
            share_gain(l)
            for q in (0, 1):
                await_weight(l, q)
                share(l, q)

        @pl.when(i == opp)
        def _():
            await_gain(l)
            share_gain(l)
            for q in (0, 2, 1, 3):
                await_weight(l, q)
                share(l, q)

    own_local = pltpu.make_async_copy(w.at[0], wbuf.at[sec], wloc)
    own_local.start()
    gbuf[sec] = gown[...]

    own_gain(0, yp).start()
    own_gain(1, ym).start()
    send_up(0)
    send_down(2)

    @pl.when(y != 1)
    def _():
        send_up(2)

    @pl.when(y != 3)
    def _():
        send_down(0)

    own_gain(2, sib).start()
    for q in range(QS):
        own_weight(2, q, sib).start()

    NPK, RIM = 5, 6

    def hand_over(some):
        @pl.when(moves)
        def _():
            for i in some:
                remote(*red[i], red_s.at[i], red_r.at[i], to).start()

        @pl.when(stay)
        def _():
            for i in some:
                pltpu.make_async_copy(*red[i], red_r.at[i]).start()

    hand_over((0, 1, 2))
    trow, tcol = rows[pl.ds(sec, 1), :], cols[pl.ds(sec, 1), :]
    lane = lax.broadcasted_iota(I32, (1, 8), 1)
    tlive = jnp.sum(jnp.where(lane == sec, live[...], 0), axis=1, keepdims=True)
    alive = lax.broadcasted_iota(I32, (1, SLOTS), 1) < tlive
    get_tiles.wait()

    def dense(r, cc):
        coef = jnp.where((trow == r) & (tcol == cc) & alive, 1.0, 0.0).astype(F32)
        total = coef[:, 0:1] * tbuf[0].astype(F32)
        for k in range(1, SLOTS):
            total = total + coef[:, k : k + 1] * tbuf[k].astype(F32)
        return total.astype(BF16)

    inner, outer = 2 * sh + 1 - tc, 2 * sh + tc
    pk[:, 0:T] = dense(outer, inner)
    pk[:, T : 2 * T] = dense(outer, outer)
    pk[:, 2 * T : 3 * T] = dense(2 * sh - 1 + 3 * tc, outer)
    fk[:, 0:T] = dense(inner, inner)
    fk[:, T : 2 * T] = dense(inner, outer)
    rk[...] = dense(2 * sh + 2 - 3 * tc, inner)

    hand_over((3, 4))

    give_far = remote(pk, npk, red_s.at[NPK], red_r.at[NPK], to_nb)
    give_rim = remote(rk, ain, red_s.at[RIM], red_r.at[RIM], to_sib)

    @pl.when(far_moves)
    def _():
        give_far.start()

    @pl.when(far_stays)
    def _():
        pltpu.make_async_copy(pk, npk, red_r.at[NPK]).start()

    @pl.when(rim_moves)
    def _():
        give_rim.start()

    @pl.when(jnp.logical_not(rim_moves))
    def _():
        pltpu.make_async_copy(rk, ain, red_r.at[RIM]).start()

    def await_red(i, dst):
        pltpu.make_async_copy(dst, dst, red_r.at[i]).wait()

    @pl.when(jnp.logical_not(joined))
    def _():
        npk[...] = jnp.zeros((T, 3 * T), BF16)
        hn[...] = jnp.zeros((2, 2 * T, D), BF16)

    inn, out_ = pl.ds(0, T), pl.ds(T, T)

    def send_inner(level):
        k = lax.rem(level, 2)
        return remote(sbuf.at[lax.rem(level, 4), inn], hs.at[k], h_s.at[k], h_r.at[k], sib)

    def send_across(step, p):
        k = lax.rem(step, 2)
        rs = pl.ds(p * T, T)
        return remote(sbuf.at[2 * k, rs], hn.at[k, rs], n_s.at[k, p], n_r.at[k, p], nb)

    def cross(step, p, what):
        @pl.when(joined)
        def _():
            if what == "go":
                send_across(step, p).start()
            else:
                send_across(step, p).wait()

    await_red(0, mbuf)
    kinds = lax.broadcasted_iota(I32, (T, 256), 0)
    hot = jnp.where(kinds == mbuf[0:1, :], 1.0, 0.0).astype(F32).T
    embedded = hot[:, 0:1] * table[0:1, :]
    for k in range(1, 4):
        embedded = embedded + hot[:, k : k + 1] * table[k : k + 1, :]
    emb[...] = embedded

    ro, ri = pl.ds(pl.multiple_of(c * T, T), T), pl.ds(pl.multiple_of((1 - c) * T, T), T)
    await_red(1, fbuf.at[ro])
    sbuf[0, out_, :] = (fbuf[ro, :].astype(F32) + emb[ro, :]).astype(BF16)
    cross(0, 1, "go")
    relay(0)
    await_red(2, fbuf.at[ri])
    sbuf[0, inn, :] = (fbuf[ri, :].astype(F32) + emb[ri, :]).astype(BF16)
    cross(0, 0, "go")
    send_inner(0).start()
    relay(1)

    @pl.when(y == 1)
    def _():
        send_up(2)

    @pl.when(y == 3)
    def _():
        send_down(0)

    await_red(3, opk)
    await_red(4, acat.at[pl.ds(0, T)])
    acat[T : 2 * T, :] = opk[:, 0 : 2 * T]
    service(0)
    own_local.wait()
    await_red(RIM, ain)

    @pl.when(joined)
    def _():
        await_red(NPK, npk)

    def other_weight(l):
        await_gain(l)
        for q in range(QS):
            await_weight(l, q)

    def update(l, aggregate, before):
        projected = dot(aggregate.astype(BF16), wbuf[l])
        scale = lax.rsqrt(jnp.mean(projected * projected, axis=-1, keepdims=True) + 1e-6)
        h = (projected * scale) * gbuf[l][0:1, :]
        gate = jnp.tanh(h * (G1 + G3 * (h * h)))
        return (before.astype(F32) + (h + h * gate)).astype(BF16)

    def two_layers(i, k, final):
        l = 2 * i
        a, b, n = 2 * k, 2 * k + 1, 2 - 2 * k

        def go(p):
            if final is None:
                cross(i + 1, p, "go")
                if p == 0:
                    send_inner(l + 2).start()
            else:
                @pl.when(final)
                def _():
                    cross(i + 1, p, "go")
                    if p == 0:
                        send_inner(l + 2).start()

        def near_outer():
            sbuf[b, out_, :] = update(
                l, own[out_, :] + dot(npk[:, 2 * T : 3 * T], hn[k, out_, :]), sbuf[a, out_, :]
            )

        def far_outer(sl, p):
            hb[...] = update(l, pre[...] + dot(npk[:, sl], hn[k, p, :]), hn[k, out_, :])

        def both_outer():
            tiles2 = jnp.concatenate([npk[:, 2 * T : 3 * T], npk[:, T : 2 * T]], axis=0)
            received = hn[k, out_, :]
            more = dot(tiles2, received)
            aggregate = more + jnp.concatenate([own[out_, :], pre[...]], axis=0)
            new = update(l, aggregate, jnp.concatenate([sbuf[a, out_, :], received], axis=0))
            sbuf[b, out_, :] = new[0:T]
            hb[...] = new[T : 2 * T]

        def next_inner():
            sbuf[n, inn, :] = update(
                l + 1, dot(acat[inn, :], sbuf[b]) + dot(ain[...], hs[1]), sbuf[b, inn, :]
            )
            go(0)

        def next_outer():
            sbuf[n, out_, :] = update(
                l + 1, dot(acat[out_, :], sbuf[b]) + dot(npk[:, 2 * T : 3 * T], hb[...]), sbuf[b, out_, :]
            )
            go(1)

        own[...] = dot(acat[...], sbuf[a])

        @pl.when(c == 1)
        def _():
            other_weight(l)

        send_inner(l).wait()
        sbuf[b, inn, :] = update(l, own[inn, :] + dot(ain[...], hs[0]), sbuf[a, inn, :])
        send_inner(l + 1).start()

        def second_weight():
            @pl.when(c == 0)
            def _():
                other_weight(l + 1)

        left, right = slice(0, T), slice(T, 2 * T)
        if k == 1:
            cross(i, 0, "take")
            pre[...] = dot(opk[:, 2 * T : 3 * T], sbuf[a, out_, :]) + dot(npk[:, left], hn[k, inn, :])
            cross(i, 1, "take")
            both_outer()
            second_weight()
            next_outer()
            send_inner(l + 1).wait()
            next_inner()
        else:
            cross(i, 1, "take")
            near_outer()
            second_weight()
            send_inner(l + 1).wait()
            next_inner()
            pre[...] = dot(opk[:, 2 * T : 3 * T], sbuf[a, out_, :]) + dot(npk[:, right], hn[k, out_, :])
            cross(i, 0, "take")
            far_outer(left, inn)
            next_outer()

    def four_layers(j, carry):
        two_layers(2 * j, 0, None)
        service(2 * j + 1)
        two_layers(2 * j + 1, 1, j < LAYERS // 4 - 1)

        @pl.when(j < LAYERS // 4 - 1)
        def _():
            service(2 * j + 2)

        return carry

    lax.fori_loop(0, LAYERS // 4, four_layers, 0)

    last = sbuf[0]
    weight = jnp.broadcast_to(head[...], (8, D))
    top = weight.astype(BF16)
    rest = weight - top.astype(F32)
    mid = rest.astype(BF16)
    low = (rest - mid.astype(F32)).astype(BF16)

    def against(part):
        return lax.dot_general(part, last, (((1,), (1,)), ((), ())), preferred_element_type=F32)

    result = against(top) + against(mid) + against(low)
    obuf[1 - c] = result[:, 0:T]
    obuf[c] = result[:, T : 2 * T]

    @pl.when(moves)
    def _():
        give = remote(obuf, rbuf, o_s, o_r, back)
        give.start()
        give.wait_send()

    @pl.when(stay)
    def _():
        pltpu.make_async_copy(obuf, rbuf, o_r).start()

    for k, dev in enumerate((yp, ym, sib)):
        own_gain(k, dev).wait_send()

    for k, dev in enumerate((yp, ym, sib)):
        for q in range(QS):
            own_weight(k, q, dev).wait_send()

    forward_gain(lm, grel_s.at[0], yp).wait_send()
    for q in (0, 1):
        forward(lm, q, rel_s.at[q], yp).wait_send()
        forward(lp, q + 2, rel_s.at[q + 2], ym).wait_send()
    for l in (lm, lp, l2):
        forward_gain(l, gfw_s.at[l], sib).wait_send()
        for q in range(QS):
            forward(l, q, fw_s.at[l, q], sib).wait_send()

    @pl.when(moves)
    def _():
        for i, (src, dst) in enumerate(red):
            remote(src, dst, red_s.at[i], red_r.at[i], to).wait_send()

    @pl.when(far_moves)
    def _():
        give_far.wait_send()

    @pl.when(rim_moves)
    def _():
        give_rim.wait_send()

    pltpu.make_async_copy(rbuf, rbuf, o_r).wait()
    out[0:1, 0:T] = rbuf[0, 0:1, :]
    out[0:1, T : 2 * T] = rbuf[1, 0:1, :]


def body(features, labels, label_table, tiles, tile_rows, tile_cols, tile_live, weights, gains, head_weight):
    vmem = pl.BlockSpec(memory_space=pltpu.VMEM)
    far = pl.BlockSpec(memory_space=pl.ANY)
    dma = pltpu.SemaphoreType.DMA
    return pl.pallas_call(
        kernel,
        out_shape=jax.ShapeDtypeStruct((1, 2 * T), F32),
        in_specs=[far] * 10,
        out_specs=vmem,
        scratch_shapes=[
            pltpu.VMEM((8, 256), I32),
            pltpu.VMEM((4, D), F32),
            pltpu.VMEM((8, SLOTS), I32),
            pltpu.VMEM((8, SLOTS), I32),
            pltpu.VMEM((1, 8), I32),
            pltpu.VMEM((1, D), BF16),
            pltpu.VMEM((1, D), F32),
            dma((7,)),
            pltpu.VMEM((2 * T, D), BF16),
            pltpu.VMEM((SLOTS, T, T), BF16),
            pltpu.VMEM((8, 256), I32),
            pltpu.VMEM((8, 256), I32),
            pltpu.VMEM((8, D), F32),
            pltpu.VMEM((LAYERS, 8, D), F32),
            pltpu.VMEM((LAYERS, D, D), BF16),
            pltpu.VMEM((4, 2 * T, D), BF16),
            pltpu.VMEM((2, T, D), BF16),
            pltpu.VMEM((2, 2 * T, D), BF16),
            pltpu.VMEM((2 * T, 2 * T), BF16),
            pltpu.VMEM((T, 3 * T), BF16),
            pltpu.VMEM((T, 2 * T), BF16),
            pltpu.VMEM((T, T), BF16),
            pltpu.VMEM((T, 3 * T), BF16),
            pltpu.VMEM((T, 3 * T), BF16),
            pltpu.VMEM((T, T), BF16),
            pltpu.VMEM((2 * T, D), F32),
            pltpu.VMEM((2 * T, D), F32),
            pltpu.VMEM((T, D), F32),
            pltpu.VMEM((T, D), BF16),
            pltpu.VMEM((2, 8, T), F32),
            pltpu.VMEM((2, 8, T), F32),
            dma((7,)),
            dma((7,)),
            dma,
            dma((3, QS)),
            dma((3,)),
            dma((LAYERS, QS)),
            dma((LAYERS,)),
            dma((QS,)),
            dma((1,)),
            dma((LAYERS, QS)),
            dma((LAYERS,)),
            dma,
            dma((2,)),
            dma((2,)),
            dma((2, 2)),
            dma((2, 2)),
            dma,
            dma,
        ],
        compiler_params=pltpu.CompilerParams(collective_id=0, has_side_effects=True),
    )(
        features, labels, label_table, tiles, tile_rows, tile_cols, tile_live.reshape(1, 8), weights, gains,
        head_weight.reshape(1, D),
    )


def solution(mesh):
    return jax.shard_map(
        body,
        mesh=mesh,
        in_specs=(
            P(None, "shard", None),
            P(None, "shard"),
            P(),
            P(None, "shard", None, None),
            P(None, "shard"),
            P(None, "shard"),
            P(None, "shard"),
            P("section", None, None),
            P("section", None),
            P(),
        ),
        out_specs=P("section", "shard"),
        check_vma=False,
    )
```

```python
import jax
import jax.numpy as jnp
from jax import lax
from jax.experimental import pallas as pl
from jax.experimental.pallas import tpu as pltpu
from jax.sharding import PartitionSpec as P

F32, BF16, I32 = jnp.float32, jnp.bfloat16, jnp.int32
T = 128
D = 512
Q = 128
QS = 4
LAYERS = 8
SLOTS = 6
YN = 4
XN = 4
CHAIN = 32
G1 = 2.0 * (2.0 / 3.141592653589793) ** 0.5
G3 = 4.0 * 0.044715 * G1


def dot(a, b):
    return jnp.dot(a, b, preferred_element_type=F32)


def remote(src, dst, send, recv, dev):
    return pltpu.make_async_remote_copy(
        src_ref=src,
        dst_ref=dst,
        send_sem=send,
        recv_sem=recv,
        device_id=dev,
        device_id_type=pl.DeviceIdType.MESH,
    )


def split(dev):
    sec, sh = dev
    return lax.div(sec, 2), lax.rem(sec, 2), lax.div(sh, XN), lax.rem(sh, XN)


def along(z, hi, f):
    return 2 * hi + jnp.where(lax.rem(z + hi, 2) == 0, f, 1 - f)


def work_of(dev):
    y, c, z, x = split(dev)
    hi, xl = lax.div(x, 2), lax.rem(x, 2)
    f = jnp.where(lax.rem(z + hi, 2) == 0, xl, 1 - xl)
    return 2 * y + hi, XN * z + 2 * f + c


def worker(dev):
    y, c, z, x = split(dev)
    return 2 * y + lax.rem(x, 2), XN * z + along(z, c, lax.div(x, 2))


def other_core(dev):
    y, c, z, x = split(dev)
    return 2 * y + 1 - c, dev[1]


def across(dev):
    y, c, z, x = split(dev)
    hi = lax.div(x, 2)
    place = lax.div(work_of(dev)[1], 2) + 2 * c - 1
    joined = (place >= 0) & (place < CHAIN)
    place = lax.rem(place + CHAIN, CHAIN)
    oz, of = lax.div(place, 2), lax.rem(place, 2)
    return (2 * y + 1 - c, XN * oz + along(oz, hi, of)), joined


def same(p, q):
    return (p[0] == q[0]) & (p[1] == q[1])


def kernel(
    feat, labels_h, table_h, tiles, rows_h, cols_h, live_h, w, gains_h, head_h,
    out,
    labels, table, rows, cols, live, gains, head, in_s,
    fbuf, tbuf, mown, mbuf, gown, gbuf, wbuf, sbuf, hs, hn, acat, pk, fk, rk, opk, npk, ain,
    emb, own, pre, hb,
    obuf, rbuf,
    red_s, red_r, wloc, os_s, gos_s, w_r, g_r, rel_s, grel_s, fw_s, gfw_s, t_s, h_s, h_r,
    n_s, n_r, o_s, o_r,
):
    sec = lax.axis_index("section")
    sh = lax.axis_index("shard")
    me = (sec, sh)
    y, c, z, x = split(me)
    sib = other_core(me)
    nb, joined = across(me)
    up = lax.rem(y + 1, YN)
    down = lax.rem(y + YN - 1, YN)
    opp = lax.rem(y + 2, YN)
    yp = (2 * up + c, sh)
    ym = (2 * down + c, sh)
    to = worker(me)
    to_sib = other_core(to)
    to_nb, to_joined = across(to)
    back, back_sib, back_nb = work_of(me), work_of(sib), work_of(nb)
    moves = jnp.logical_not(same(to, me))
    stay = same(to, me)
    rim_moves = jnp.logical_not(same(to_sib, me))
    far_moves = to_joined & jnp.logical_not(same(to_nb, me))
    far_stays = to_joined & same(to_nb, me)
    far_comes = joined & jnp.logical_not(same(back_nb, me))

    small = (
        (labels_h, labels), (rows_h, rows), (cols_h, cols), (live_h, live), (gains_h, gains),
        (table_h, table), (head_h, head),
    )
    fetches = [pltpu.make_async_copy(src, dst, in_s.at[i]) for i, (src, dst) in enumerate(small)]
    for fetch in fetches:
        fetch.start()
    get_tiles = pltpu.make_async_copy(tiles.at[sec], tbuf, t_s)
    get_tiles.start()

    barrier = pltpu.get_barrier_semaphore()

    def greet(*devs):
        for dev in devs:
            pl.semaphore_signal(barrier, inc=1, device_id=dev, device_id_type=pl.DeviceIdType.MESH)

    greet(sib, yp, ym)

    @pl.when(joined)
    def _():
        greet(nb)

    @pl.when(moves)
    def _():
        greet(to, back)

    @pl.when(rim_moves)
    def _():
        greet(to_sib, back_sib)

    @pl.when(far_moves)
    def _():
        greet(to_nb)

    @pl.when(far_comes)
    def _():
        greet(back_nb)

    for fetch in fetches:
        fetch.wait()

    mown[...] = jnp.broadcast_to(labels[pl.ds(sec, 1), :], (8, 256))
    gown[...] = jnp.broadcast_to(0.5 * gains[...].astype(F32), (8, D))
    amount = jnp.where(moves, 2, 0) + jnp.where(rim_moves, 2, 0) + jnp.where(far_moves, 1, 0)
    amount = amount + jnp.where(far_comes, 1, 0) + jnp.where(joined, 1, 0)
    pl.semaphore_wait(barrier, 3 + amount)

    tc = lax.rem(x, 2)
    fo, fi = pl.ds(pl.multiple_of(tc * T, T), T), pl.ds(pl.multiple_of((1 - tc) * T, T), T)
    red = (
        (mown, mbuf), (feat.at[sec, fo], fbuf.at[fo]), (feat.at[sec, fi], fbuf.at[fi]),
        (pk, opk), (fk, acat.at[pl.ds(0, T)]),
    )
    def part(q):
        return pl.ds(q * Q, Q)

    def own_weight(k, q, dev):
        return remote(w.at[0, part(q)], wbuf.at[sec, part(q)], os_s.at[k, q], w_r.at[sec, q], dev)

    def own_gain(k, dev):
        return remote(gown, gbuf.at[sec], gos_s.at[k], g_r.at[sec], dev)

    def forward(l, q, send, dev):
        return remote(wbuf.at[l, part(q)], wbuf.at[l, part(q)], send, w_r.at[l, q], dev)

    def forward_gain(l, send, dev):
        return remote(gbuf.at[l], gbuf.at[l], send, g_r.at[l], dev)

    def await_weight(l, q):
        pltpu.make_async_copy(wbuf.at[l, part(q)], wbuf.at[l, part(q)], w_r.at[l, q]).wait()

    def await_gain(l):
        pltpu.make_async_copy(gbuf.at[l], gbuf.at[l], g_r.at[l]).wait()

    lm, lp, l2 = 2 * down + c, 2 * up + c, 2 * opp + c

    def send_up(q):
        for k in (q, q + 1):
            own_weight(0, k, yp).start()

    def send_down(q):
        for k in (q, q + 1):
            own_weight(1, k, ym).start()

    def share(l, q):
        forward(l, q, fw_s.at[l, q], sib).start()

    def share_gain(l):
        forward_gain(l, gfw_s.at[l], sib).start()

    def relay(q):
        if q == 0:
            await_gain(lm)
            forward_gain(lm, grel_s.at[0], yp).start()
            share_gain(lm)
        await_weight(lm, q)
        forward(lm, q, rel_s.at[q], yp).start()
        await_weight(lp, q + 2)
        forward(lp, q + 2, rel_s.at[q + 2], ym).start()
        share(lm, q)
        share(lp, q + 2)

    def service(i):
        l = 2 * i + c

        @pl.when(i == down)
        def _():
            for q in (2, 3):
                await_weight(l, q)
                share(l, q)

        @pl.when(i == up)
        def _():
            await_gain(l)
            share_gain(l)
            for q in (0, 1):
                await_weight(l, q)
                share(l, q)

        @pl.when(i == opp)
        def _():
            await_gain(l)
            share_gain(l)
            for q in (0, 2, 1, 3):
                await_weight(l, q)
                share(l, q)

    own_local = pltpu.make_async_copy(w.at[0], wbuf.at[sec], wloc)
    own_local.start()
    gbuf[sec] = gown[...]

    own_gain(0, yp).start()
    own_gain(1, ym).start()
    send_up(0)
    send_down(2)

    @pl.when(y != 1)
    def _():
        send_up(2)

    @pl.when(y != 3)
    def _():
        send_down(0)

    own_gain(2, sib).start()
    for q in range(QS):
        own_weight(2, q, sib).start()

    NPK, RIM = 5, 6

    def hand_over(some):
        @pl.when(moves)
        def _():
            for i in some:
                remote(*red[i], red_s.at[i], red_r.at[i], to).start()

        @pl.when(stay)
        def _():
            for i in some:
                pltpu.make_async_copy(*red[i], red_r.at[i]).start()

    hand_over((0, 1, 2))
    trow, tcol = rows[pl.ds(sec, 1), :], cols[pl.ds(sec, 1), :]
    lane = lax.broadcasted_iota(I32, (1, 8), 1)
    tlive = jnp.sum(jnp.where(lane == sec, live[...], 0), axis=1, keepdims=True)
    alive = lax.broadcasted_iota(I32, (1, SLOTS), 1) < tlive
    get_tiles.wait()

    def dense(r, cc):
        coef = jnp.where((trow == r) & (tcol == cc) & alive, 1.0, 0.0).astype(F32)
        total = coef[:, 0:1] * tbuf[0].astype(F32)
        for k in range(1, SLOTS):
            total = total + coef[:, k : k + 1] * tbuf[k].astype(F32)
        return total.astype(BF16)

    inner, outer = 2 * sh + 1 - tc, 2 * sh + tc
    pk[:, 0:T] = dense(outer, inner)
    pk[:, T : 2 * T] = dense(outer, outer)
    pk[:, 2 * T : 3 * T] = dense(2 * sh - 1 + 3 * tc, outer)
    fk[:, 0:T] = dense(inner, inner)
    fk[:, T : 2 * T] = dense(inner, outer)
    rk[...] = dense(2 * sh + 2 - 3 * tc, inner)

    hand_over((3, 4))

    give_far = remote(pk, npk, red_s.at[NPK], red_r.at[NPK], to_nb)
    give_rim = remote(rk, ain, red_s.at[RIM], red_r.at[RIM], to_sib)

    @pl.when(far_moves)
    def _():
        give_far.start()

    @pl.when(far_stays)
    def _():
        pltpu.make_async_copy(pk, npk, red_r.at[NPK]).start()

    @pl.when(rim_moves)
    def _():
        give_rim.start()

    @pl.when(jnp.logical_not(rim_moves))
    def _():
        pltpu.make_async_copy(rk, ain, red_r.at[RIM]).start()

    def await_red(i, dst):
        pltpu.make_async_copy(dst, dst, red_r.at[i]).wait()

    @pl.when(jnp.logical_not(joined))
    def _():
        npk[...] = jnp.zeros((T, 3 * T), BF16)
        hn[...] = jnp.zeros((2, 2 * T, D), BF16)

    inn, out_ = pl.ds(0, T), pl.ds(T, T)

    def send_inner(level):
        k = lax.rem(level, 2)
        return remote(sbuf.at[lax.rem(level, 4), inn], hs.at[k], h_s.at[k], h_r.at[k], sib)

    def send_across(step, p):
        k = lax.rem(step, 2)
        rs = pl.ds(p * T, T)
        return remote(sbuf.at[2 * k, rs], hn.at[k, rs], n_s.at[k, p], n_r.at[k, p], nb)

    def cross(step, p, what):
        @pl.when(joined)
        def _():
            if what == "go":
                send_across(step, p).start()
            else:
                send_across(step, p).wait()

    await_red(0, mbuf)
    kinds = lax.broadcasted_iota(I32, (T, 256), 0)
    hot = jnp.where(kinds == mbuf[0:1, :], 1.0, 0.0).astype(F32).T
    embedded = hot[:, 0:1] * table[0:1, :]
    for k in range(1, 4):
        embedded = embedded + hot[:, k : k + 1] * table[k : k + 1, :]
    emb[...] = embedded

    ro, ri = pl.ds(pl.multiple_of(c * T, T), T), pl.ds(pl.multiple_of((1 - c) * T, T), T)
    await_red(1, fbuf.at[ro])
    sbuf[0, out_, :] = (fbuf[ro, :].astype(F32) + emb[ro, :]).astype(BF16)
    cross(0, 1, "go")
    relay(0)
    await_red(2, fbuf.at[ri])
    sbuf[0, inn, :] = (fbuf[ri, :].astype(F32) + emb[ri, :]).astype(BF16)
    cross(0, 0, "go")
    send_inner(0).start()
    relay(1)

    @pl.when(y == 1)
    def _():
        send_up(2)

    @pl.when(y == 3)
    def _():
        send_down(0)

    await_red(3, opk)
    await_red(4, acat.at[pl.ds(0, T)])
    acat[T : 2 * T, :] = opk[:, 0 : 2 * T]
    service(0)
    own_local.wait()
    await_red(RIM, ain)

    @pl.when(joined)
    def _():
        await_red(NPK, npk)

    def other_weight(l):
        await_gain(l)
        for q in range(QS):
            await_weight(l, q)

    def update(l, aggregate, before):
        projected = dot(aggregate.astype(BF16), wbuf[l])
        scale = lax.rsqrt(jnp.mean(projected * projected, axis=-1, keepdims=True) + 1e-6)
        h = (projected * scale) * gbuf[l][0:1, :]
        gate = jnp.tanh(h * (G1 + G3 * (h * h)))
        return (before.astype(F32) + (h + h * gate)).astype(BF16)

    def two_layers(i, k, final):
        l = 2 * i
        a, b, n = 2 * k, 2 * k + 1, 2 - 2 * k

        def go(p):
            if final is None:
                cross(i + 1, p, "go")
                if p == 0:
                    send_inner(l + 2).start()
            else:
                @pl.when(final)
                def _():
                    cross(i + 1, p, "go")
                    if p == 0:
                        send_inner(l + 2).start()

        def near_outer():
            sbuf[b, out_, :] = update(
                l, own[out_, :] + dot(npk[:, 2 * T : 3 * T], hn[k, out_, :]), sbuf[a, out_, :]
            )

        def far_outer(sl, p):
            hb[...] = update(l, pre[...] + dot(npk[:, sl], hn[k, p, :]), hn[k, out_, :])

        def both_outer():
            tiles2 = jnp.concatenate([npk[:, 2 * T : 3 * T], npk[:, T : 2 * T]], axis=0)
            received = hn[k, out_, :]
            more = dot(tiles2, received)
            aggregate = more + jnp.concatenate([own[out_, :], pre[...]], axis=0)
            new = update(l, aggregate, jnp.concatenate([sbuf[a, out_, :], received], axis=0))
            sbuf[b, out_, :] = new[0:T]
            hb[...] = new[T : 2 * T]

        def next_inner():
            sbuf[n, inn, :] = update(
                l + 1, dot(acat[inn, :], sbuf[b]) + dot(ain[...], hs[1]), sbuf[b, inn, :]
            )
            go(0)

        def next_outer():
            sbuf[n, out_, :] = update(
                l + 1, dot(acat[out_, :], sbuf[b]) + dot(npk[:, 2 * T : 3 * T], hb[...]), sbuf[b, out_, :]
            )
            go(1)

        own[...] = dot(acat[...], sbuf[a])

        @pl.when(c == 1)
        def _():
            other_weight(l)

        send_inner(l).wait()
        sbuf[b, inn, :] = update(l, own[inn, :] + dot(ain[...], hs[0]), sbuf[a, inn, :])
        send_inner(l + 1).start()

        def second_weight():
            @pl.when(c == 0)
            def _():
                other_weight(l + 1)

        left, right = slice(0, T), slice(T, 2 * T)
        if k == 0:
            cross(i, 0, "take")
            pre[...] = dot(opk[:, 2 * T : 3 * T], sbuf[a, out_, :]) + dot(npk[:, left], hn[k, inn, :])
            cross(i, 1, "take")
            both_outer()
            second_weight()
            next_outer()
            send_inner(l + 1).wait()
            next_inner()
        else:
            cross(i, 1, "take")
            near_outer()
            second_weight()
            send_inner(l + 1).wait()
            next_inner()
            pre[...] = dot(opk[:, 2 * T : 3 * T], sbuf[a, out_, :]) + dot(npk[:, right], hn[k, out_, :])
            cross(i, 0, "take")
            far_outer(left, inn)
            next_outer()

    def four_layers(j, carry):
        two_layers(2 * j, 0, None)
        service(2 * j + 1)
        two_layers(2 * j + 1, 1, j < LAYERS // 4 - 1)

        @pl.when(j < LAYERS // 4 - 1)
        def _():
            service(2 * j + 2)

        return carry

    lax.fori_loop(0, LAYERS // 4, four_layers, 0)

    last = sbuf[0]
    weight = jnp.broadcast_to(head[...], (8, D))
    top = weight.astype(BF16)
    rest = weight - top.astype(F32)
    mid = rest.astype(BF16)
    low = (rest - mid.astype(F32)).astype(BF16)

    def against(part):
        return lax.dot_general(part, last, (((1,), (1,)), ((), ())), preferred_element_type=F32)

    result = against(top) + against(mid) + against(low)
    obuf[1 - c] = result[:, 0:T]
    obuf[c] = result[:, T : 2 * T]

    @pl.when(moves)
    def _():
        give = remote(obuf, rbuf, o_s, o_r, back)
        give.start()
        give.wait_send()

    @pl.when(stay)
    def _():
        pltpu.make_async_copy(obuf, rbuf, o_r).start()

    for k, dev in enumerate((yp, ym, sib)):
        own_gain(k, dev).wait_send()

    for k, dev in enumerate((yp, ym, sib)):
        for q in range(QS):
            own_weight(k, q, dev).wait_send()

    forward_gain(lm, grel_s.at[0], yp).wait_send()
    for q in (0, 1):
        forward(lm, q, rel_s.at[q], yp).wait_send()
        forward(lp, q + 2, rel_s.at[q + 2], ym).wait_send()
    for l in (lm, lp, l2):
        forward_gain(l, gfw_s.at[l], sib).wait_send()
        for q in range(QS):
            forward(l, q, fw_s.at[l, q], sib).wait_send()

    @pl.when(moves)
    def _():
        for i, (src, dst) in enumerate(red):
            remote(src, dst, red_s.at[i], red_r.at[i], to).wait_send()

    @pl.when(far_moves)
    def _():
        give_far.wait_send()

    @pl.when(rim_moves)
    def _():
        give_rim.wait_send()

    pltpu.make_async_copy(rbuf, rbuf, o_r).wait()
    out[0:1, 0:T] = rbuf[0, 0:1, :]
    out[0:1, T : 2 * T] = rbuf[1, 0:1, :]


def body(features, labels, label_table, tiles, tile_rows, tile_cols, tile_live, weights, gains, head_weight):
    vmem = pl.BlockSpec(memory_space=pltpu.VMEM)
    far = pl.BlockSpec(memory_space=pl.ANY)
    dma = pltpu.SemaphoreType.DMA
    return pl.pallas_call(
        kernel,
        out_shape=jax.ShapeDtypeStruct((1, 2 * T), F32),
        in_specs=[far] * 10,
        out_specs=vmem,
        scratch_shapes=[
            pltpu.VMEM((8, 256), I32),
            pltpu.VMEM((4, D), F32),
            pltpu.VMEM((8, SLOTS), I32),
            pltpu.VMEM((8, SLOTS), I32),
            pltpu.VMEM((1, 8), I32),
            pltpu.VMEM((1, D), BF16),
            pltpu.VMEM((1, D), F32),
            dma((7,)),
            pltpu.VMEM((2 * T, D), BF16),
            pltpu.VMEM((SLOTS, T, T), BF16),
            pltpu.VMEM((8, 256), I32),
            pltpu.VMEM((8, 256), I32),
            pltpu.VMEM((8, D), F32),
            pltpu.VMEM((LAYERS, 8, D), F32),
            pltpu.VMEM((LAYERS, D, D), BF16),
            pltpu.VMEM((4, 2 * T, D), BF16),
            pltpu.VMEM((2, T, D), BF16),
            pltpu.VMEM((2, 2 * T, D), BF16),
            pltpu.VMEM((2 * T, 2 * T), BF16),
            pltpu.VMEM((T, 3 * T), BF16),
            pltpu.VMEM((T, 2 * T), BF16),
            pltpu.VMEM((T, T), BF16),
            pltpu.VMEM((T, 3 * T), BF16),
            pltpu.VMEM((T, 3 * T), BF16),
            pltpu.VMEM((T, T), BF16),
            pltpu.VMEM((2 * T, D), F32),
            pltpu.VMEM((2 * T, D), F32),
            pltpu.VMEM((T, D), F32),
            pltpu.VMEM((T, D), BF16),
            pltpu.VMEM((2, 8, T), F32),
            pltpu.VMEM((2, 8, T), F32),
            dma((7,)),
            dma((7,)),
            dma,
            dma((3, QS)),
            dma((3,)),
            dma((LAYERS, QS)),
            dma((LAYERS,)),
            dma((QS,)),
            dma((1,)),
            dma((LAYERS, QS)),
            dma((LAYERS,)),
            dma,
            dma((2,)),
            dma((2,)),
            dma((2, 2)),
            dma((2, 2)),
            dma,
            dma,
        ],
        compiler_params=pltpu.CompilerParams(collective_id=0, has_side_effects=True),
    )(
        features, labels, label_table, tiles, tile_rows, tile_cols, tile_live.reshape(1, 8), weights, gains,
        head_weight.reshape(1, D),
    )


def solution(mesh):
    return jax.shard_map(
        body,
        mesh=mesh,
        in_specs=(
            P(None, "shard", None),
            P(None, "shard"),
            P(),
            P(None, "shard", None, None),
            P(None, "shard"),
            P(None, "shard"),
            P(None, "shard"),
            P("section", None, None),
            P("section", None),
            P(),
        ),
        out_specs=P("section", "shard"),
        check_vma=False,
    )
```

```python
import jax
import jax.numpy as jnp
from jax import lax
from jax.experimental import pallas as pl
from jax.experimental.pallas import tpu as pltpu
from jax.sharding import PartitionSpec as P

F32, BF16, I32 = jnp.float32, jnp.bfloat16, jnp.int32
T = 128
D = 512
Q = 128
QS = 4
LAYERS = 8
SLOTS = 6
YN = 4
XN = 4
CHAIN = 32
G1 = 2.0 * (2.0 / 3.141592653589793) ** 0.5
G3 = 4.0 * 0.044715 * G1


def dot(a, b):
    return jnp.dot(a, b, preferred_element_type=F32)


def remote(src, dst, send, recv, dev):
    return pltpu.make_async_remote_copy(
        src_ref=src,
        dst_ref=dst,
        send_sem=send,
        recv_sem=recv,
        device_id=dev,
        device_id_type=pl.DeviceIdType.MESH,
    )


def split(dev):
    sec, sh = dev
    return lax.div(sec, 2), lax.rem(sec, 2), lax.div(sh, XN), lax.rem(sh, XN)


def along(z, hi, f):
    return 2 * hi + jnp.where(lax.rem(z + hi, 2) == 0, f, 1 - f)


def work_of(dev):
    y, c, z, x = split(dev)
    hi, xl = lax.div(x, 2), lax.rem(x, 2)
    f = jnp.where(lax.rem(z + hi, 2) == 0, xl, 1 - xl)
    return 2 * y + hi, XN * z + 2 * f + c


def worker(dev):
    y, c, z, x = split(dev)
    return 2 * y + lax.rem(x, 2), XN * z + along(z, c, lax.div(x, 2))


def other_core(dev):
    y, c, z, x = split(dev)
    return 2 * y + 1 - c, dev[1]


def across(dev):
    y, c, z, x = split(dev)
    hi = lax.div(x, 2)
    place = lax.div(work_of(dev)[1], 2) + 2 * c - 1
    joined = (place >= 0) & (place < CHAIN)
    place = lax.rem(place + CHAIN, CHAIN)
    oz, of = lax.div(place, 2), lax.rem(place, 2)
    return (2 * y + 1 - c, XN * oz + along(oz, hi, of)), joined


def same(p, q):
    return (p[0] == q[0]) & (p[1] == q[1])


def kernel(
    feat, labels_h, table_h, tiles, rows_h, cols_h, live_h, w, gains_h, head_h,
    out,
    labels, table, rows, cols, live, gains, head, in_s,
    fbuf, tbuf, mown, mbuf, gown, gbuf, wbuf, sbuf, hs, hn, acat, pk, fk, rk, opk, npk, ain,
    emb, own, pre, hb,
    obuf, rbuf,
    red_s, red_r, wloc, os_s, gos_s, w_r, g_r, rel_s, grel_s, fw_s, gfw_s, t_s, h_s, h_r,
    n_s, n_r, o_s, o_r,
):
    sec = lax.axis_index("section")
    sh = lax.axis_index("shard")
    me = (sec, sh)
    y, c, z, x = split(me)
    sib = other_core(me)
    nb, joined = across(me)
    up = lax.rem(y + 1, YN)
    down = lax.rem(y + YN - 1, YN)
    opp = lax.rem(y + 2, YN)
    yp = (2 * up + c, sh)
    ym = (2 * down + c, sh)
    to = worker(me)
    to_sib = other_core(to)
    to_nb, to_joined = across(to)
    back, back_sib, back_nb = work_of(me), work_of(sib), work_of(nb)
    moves = jnp.logical_not(same(to, me))
    stay = same(to, me)
    rim_moves = jnp.logical_not(same(to_sib, me))
    far_moves = to_joined & jnp.logical_not(same(to_nb, me))
    far_stays = to_joined & same(to_nb, me)
    far_comes = joined & jnp.logical_not(same(back_nb, me))

    small = (
        (labels_h, labels), (rows_h, rows), (cols_h, cols), (live_h, live), (gains_h, gains),
        (table_h, table), (head_h, head),
    )
    fetches = [pltpu.make_async_copy(src, dst, in_s.at[i]) for i, (src, dst) in enumerate(small)]
    for fetch in fetches:
        fetch.start()
    get_tiles = pltpu.make_async_copy(tiles.at[sec], tbuf, t_s)
    get_tiles.start()

    barrier = pltpu.get_barrier_semaphore()

    def greet(*devs):
        for dev in devs:
            pl.semaphore_signal(barrier, inc=1, device_id=dev, device_id_type=pl.DeviceIdType.MESH)

    greet(sib, yp, ym)

    @pl.when(joined)
    def _():
        greet(nb)

    @pl.when(moves)
    def _():
        greet(to, back)

    @pl.when(rim_moves)
    def _():
        greet(to_sib, back_sib)

    @pl.when(far_moves)
    def _():
        greet(to_nb)

    @pl.when(far_comes)
    def _():
        greet(back_nb)

    for fetch in fetches:
        fetch.wait()

    mown[...] = jnp.broadcast_to(labels[pl.ds(sec, 1), :], (8, 256))
    gown[...] = jnp.broadcast_to(0.5 * gains[...].astype(F32), (8, D))
    amount = jnp.where(moves, 2, 0) + jnp.where(rim_moves, 2, 0) + jnp.where(far_moves, 1, 0)
    amount = amount + jnp.where(far_comes, 1, 0) + jnp.where(joined, 1, 0)
    pl.semaphore_wait(barrier, 3 + amount)

    tc = lax.rem(x, 2)
    fo, fi = pl.ds(pl.multiple_of(tc * T, T), T), pl.ds(pl.multiple_of((1 - tc) * T, T), T)
    red = (
        (mown, mbuf), (feat.at[sec, fo], fbuf.at[fo]), (feat.at[sec, fi], fbuf.at[fi]),
        (pk, opk), (fk, acat.at[pl.ds(0, T)]),
    )
    def part(q):
        return pl.ds(q * Q, Q)

    def own_weight(k, q, dev):
        return remote(w.at[0, part(q)], wbuf.at[sec, part(q)], os_s.at[k, q], w_r.at[sec, q], dev)

    def own_gain(k, dev):
        return remote(gown, gbuf.at[sec], gos_s.at[k], g_r.at[sec], dev)

    def forward(l, q, send, dev):
        return remote(wbuf.at[l, part(q)], wbuf.at[l, part(q)], send, w_r.at[l, q], dev)

    def forward_gain(l, send, dev):
        return remote(gbuf.at[l], gbuf.at[l], send, g_r.at[l], dev)

    def await_weight(l, q):
        pltpu.make_async_copy(wbuf.at[l, part(q)], wbuf.at[l, part(q)], w_r.at[l, q]).wait()

    def await_gain(l):
        pltpu.make_async_copy(gbuf.at[l], gbuf.at[l], g_r.at[l]).wait()

    lm, lp, l2 = 2 * down + c, 2 * up + c, 2 * opp + c

    def send_up(q):
        for k in (q, q + 1):
            own_weight(0, k, yp).start()

    def send_down(q):
        for k in (q, q + 1):
            own_weight(1, k, ym).start()

    def share(l, q):
        forward(l, q, fw_s.at[l, q], sib).start()

    def share_gain(l):
        forward_gain(l, gfw_s.at[l], sib).start()

    def relay(q):
        if q == 0:
            await_gain(lm)
            forward_gain(lm, grel_s.at[0], yp).start()
            share_gain(lm)
        await_weight(lm, q)
        forward(lm, q, rel_s.at[q], yp).start()
        await_weight(lp, q + 2)
        forward(lp, q + 2, rel_s.at[q + 2], ym).start()
        share(lm, q)
        share(lp, q + 2)

    def service(i):
        l = 2 * i + c

        @pl.when(i == down)
        def _():
            for q in (2, 3):
                await_weight(l, q)
                share(l, q)

        @pl.when(i == up)
        def _():
            await_gain(l)
            share_gain(l)
            for q in (0, 1):
                await_weight(l, q)
                share(l, q)

        @pl.when(i == opp)
        def _():
            await_gain(l)
            share_gain(l)
            for q in (0, 2, 1, 3):
                await_weight(l, q)
                share(l, q)

    own_local = pltpu.make_async_copy(w.at[0], wbuf.at[sec], wloc)
    own_local.start()
    gbuf[sec] = gown[...]

    own_gain(0, yp).start()
    own_gain(1, ym).start()
    send_up(0)
    send_down(2)

    late = y == 2

    @pl.when((y != 1) & jnp.logical_not(late))
    def _():
        send_up(2)

    @pl.when((y != 3) & jnp.logical_not(late))
    def _():
        send_down(0)

    own_gain(2, sib).start()
    for q in range(QS):
        own_weight(2, q, sib).start()

    NPK, RIM = 5, 6

    def hand_over(some):
        @pl.when(moves)
        def _():
            for i in some:
                remote(*red[i], red_s.at[i], red_r.at[i], to).start()

        @pl.when(stay)
        def _():
            for i in some:
                pltpu.make_async_copy(*red[i], red_r.at[i]).start()

    hand_over((0, 1, 2))
    trow, tcol = rows[pl.ds(sec, 1), :], cols[pl.ds(sec, 1), :]
    lane = lax.broadcasted_iota(I32, (1, 8), 1)
    tlive = jnp.sum(jnp.where(lane == sec, live[...], 0), axis=1, keepdims=True)
    alive = lax.broadcasted_iota(I32, (1, SLOTS), 1) < tlive
    get_tiles.wait()

    def dense(r, cc):
        coef = jnp.where((trow == r) & (tcol == cc) & alive, 1.0, 0.0).astype(F32)
        total = coef[:, 0:1] * tbuf[0].astype(F32)
        for k in range(1, SLOTS):
            total = total + coef[:, k : k + 1] * tbuf[k].astype(F32)
        return total.astype(BF16)

    inner, outer = 2 * sh + 1 - tc, 2 * sh + tc
    pk[:, 0:T] = dense(outer, inner)
    pk[:, T : 2 * T] = dense(outer, outer)
    pk[:, 2 * T : 3 * T] = dense(2 * sh - 1 + 3 * tc, outer)
    fk[:, 0:T] = dense(inner, inner)
    fk[:, T : 2 * T] = dense(inner, outer)
    rk[...] = dense(2 * sh + 2 - 3 * tc, inner)

    hand_over((3, 4))

    give_far = remote(pk, npk, red_s.at[NPK], red_r.at[NPK], to_nb)
    give_rim = remote(rk, ain, red_s.at[RIM], red_r.at[RIM], to_sib)

    @pl.when(far_moves)
    def _():
        give_far.start()

    @pl.when(far_stays)
    def _():
        pltpu.make_async_copy(pk, npk, red_r.at[NPK]).start()

    @pl.when(rim_moves)
    def _():
        give_rim.start()

    @pl.when(jnp.logical_not(rim_moves))
    def _():
        pltpu.make_async_copy(rk, ain, red_r.at[RIM]).start()

    def await_red(i, dst):
        pltpu.make_async_copy(dst, dst, red_r.at[i]).wait()

    @pl.when(jnp.logical_not(joined))
    def _():
        npk[...] = jnp.zeros((T, 3 * T), BF16)
        hn[...] = jnp.zeros((2, 2 * T, D), BF16)

    inn, out_ = pl.ds(0, T), pl.ds(T, T)

    def send_inner(level):
        k = lax.rem(level, 2)
        return remote(sbuf.at[lax.rem(level, 4), inn], hs.at[k], h_s.at[k], h_r.at[k], sib)

    def send_across(step, p):
        k = lax.rem(step, 2)
        rs = pl.ds(p * T, T)
        return remote(sbuf.at[2 * k, rs], hn.at[k, rs], n_s.at[k, p], n_r.at[k, p], nb)

    def cross(step, p, what):
        @pl.when(joined)
        def _():
            if what == "go":
                send_across(step, p).start()
            else:
                send_across(step, p).wait()

    await_red(0, mbuf)
    kinds = lax.broadcasted_iota(I32, (T, 256), 0)
    hot = jnp.where(kinds == mbuf[0:1, :], 1.0, 0.0).astype(F32).T
    embedded = hot[:, 0:1] * table[0:1, :]
    for k in range(1, 4):
        embedded = embedded + hot[:, k : k + 1] * table[k : k + 1, :]
    emb[...] = embedded

    ro, ri = pl.ds(pl.multiple_of(c * T, T), T), pl.ds(pl.multiple_of((1 - c) * T, T), T)
    await_red(1, fbuf.at[ro])

    @pl.when((y != 1) & late)
    def _():
        send_up(2)

    @pl.when((y != 3) & late)
    def _():
        send_down(0)

    sbuf[0, out_, :] = (fbuf[ro, :].astype(F32) + emb[ro, :]).astype(BF16)
    cross(0, 1, "go")
    relay(0)
    await_red(2, fbuf.at[ri])
    sbuf[0, inn, :] = (fbuf[ri, :].astype(F32) + emb[ri, :]).astype(BF16)
    cross(0, 0, "go")
    send_inner(0).start()
    relay(1)

    @pl.when(y == 1)
    def _():
        send_up(2)

    @pl.when(y == 3)
    def _():
        send_down(0)

    await_red(3, opk)
    await_red(4, acat.at[pl.ds(0, T)])
    acat[T : 2 * T, :] = opk[:, 0 : 2 * T]
    service(0)
    own_local.wait()
    await_red(RIM, ain)

    @pl.when(joined)
    def _():
        await_red(NPK, npk)

    def other_weight(l):
        await_gain(l)
        for q in range(QS):
            await_weight(l, q)

    def update(l, aggregate, before):
        projected = dot(aggregate.astype(BF16), wbuf[l])
        scale = lax.rsqrt(jnp.mean(projected * projected, axis=-1, keepdims=True) + 1e-6)
        h = (projected * scale) * gbuf[l][0:1, :]
        gate = jnp.tanh(h * (G1 + G3 * (h * h)))
        return (before.astype(F32) + (h + h * gate)).astype(BF16)

    def two_layers(i, k, final):
        l = 2 * i
        a, b, n = 2 * k, 2 * k + 1, 2 - 2 * k

        def go(p):
            if final is None:
                cross(i + 1, p, "go")
                if p == 0:
                    send_inner(l + 2).start()
            else:
                @pl.when(final)
                def _():
                    cross(i + 1, p, "go")
                    if p == 0:
                        send_inner(l + 2).start()

        def near_outer():
            sbuf[b, out_, :] = update(
                l, own[out_, :] + dot(npk[:, 2 * T : 3 * T], hn[k, out_, :]), sbuf[a, out_, :]
            )

        def far_outer(sl, p):
            hb[...] = update(l, pre[...] + dot(npk[:, sl], hn[k, p, :]), hn[k, out_, :])

        def both_outer():
            tiles2 = jnp.concatenate([npk[:, 2 * T : 3 * T], npk[:, T : 2 * T]], axis=0)
            received = hn[k, out_, :]
            more = dot(tiles2, received)
            aggregate = more + jnp.concatenate([own[out_, :], pre[...]], axis=0)
            new = update(l, aggregate, jnp.concatenate([sbuf[a, out_, :], received], axis=0))
            sbuf[b, out_, :] = new[0:T]
            hb[...] = new[T : 2 * T]

        def next_inner():
            sbuf[n, inn, :] = update(
                l + 1, dot(acat[inn, :], sbuf[b]) + dot(ain[...], hs[1]), sbuf[b, inn, :]
            )
            go(0)

        def next_outer():
            sbuf[n, out_, :] = update(
                l + 1, dot(acat[out_, :], sbuf[b]) + dot(npk[:, 2 * T : 3 * T], hb[...]), sbuf[b, out_, :]
            )
            go(1)

        own[...] = dot(acat[...], sbuf[a])

        @pl.when(c == 1)
        def _():
            other_weight(l)

        send_inner(l).wait()
        sbuf[b, inn, :] = update(l, own[inn, :] + dot(ain[...], hs[0]), sbuf[a, inn, :])
        send_inner(l + 1).start()

        def second_weight():
            @pl.when(c == 0)
            def _():
                other_weight(l + 1)

        left, right = slice(0, T), slice(T, 2 * T)
        if k == 0:
            cross(i, 0, "take")
            pre[...] = dot(opk[:, 2 * T : 3 * T], sbuf[a, out_, :]) + dot(npk[:, left], hn[k, inn, :])
            cross(i, 1, "take")
            both_outer()
            second_weight()
            next_outer()
            send_inner(l + 1).wait()
            next_inner()
        else:
            cross(i, 1, "take")
            near_outer()
            second_weight()
            send_inner(l + 1).wait()
            next_inner()
            pre[...] = dot(opk[:, 2 * T : 3 * T], sbuf[a, out_, :]) + dot(npk[:, right], hn[k, out_, :])
            cross(i, 0, "take")
            far_outer(left, inn)
            next_outer()

    def four_layers(j, carry):
        two_layers(2 * j, 0, None)
        service(2 * j + 1)
        two_layers(2 * j + 1, 1, j < LAYERS // 4 - 1)

        @pl.when(j < LAYERS // 4 - 1)
        def _():
            service(2 * j + 2)

        return carry

    lax.fori_loop(0, LAYERS // 4, four_layers, 0)

    last = sbuf[0]
    weight = jnp.broadcast_to(head[...], (8, D))
    top = weight.astype(BF16)
    rest = weight - top.astype(F32)
    mid = rest.astype(BF16)
    low = (rest - mid.astype(F32)).astype(BF16)

    def against(part):
        return lax.dot_general(part, last, (((1,), (1,)), ((), ())), preferred_element_type=F32)

    result = against(top) + against(mid) + against(low)
    obuf[1 - c] = result[:, 0:T]
    obuf[c] = result[:, T : 2 * T]

    @pl.when(moves)
    def _():
        give = remote(obuf, rbuf, o_s, o_r, back)
        give.start()
        give.wait_send()

    @pl.when(stay)
    def _():
        pltpu.make_async_copy(obuf, rbuf, o_r).start()

    for k, dev in enumerate((yp, ym, sib)):
        own_gain(k, dev).wait_send()

    for k, dev in enumerate((yp, ym, sib)):
        for q in range(QS):
            own_weight(k, q, dev).wait_send()

    forward_gain(lm, grel_s.at[0], yp).wait_send()
    for q in (0, 1):
        forward(lm, q, rel_s.at[q], yp).wait_send()
        forward(lp, q + 2, rel_s.at[q + 2], ym).wait_send()
    for l in (lm, lp, l2):
        forward_gain(l, gfw_s.at[l], sib).wait_send()
        for q in range(QS):
            forward(l, q, fw_s.at[l, q], sib).wait_send()

    @pl.when(moves)
    def _():
        for i, (src, dst) in enumerate(red):
            remote(src, dst, red_s.at[i], red_r.at[i], to).wait_send()

    @pl.when(far_moves)
    def _():
        give_far.wait_send()

    @pl.when(rim_moves)
    def _():
        give_rim.wait_send()

    pltpu.make_async_copy(rbuf, rbuf, o_r).wait()
    out[0:1, 0:T] = rbuf[0, 0:1, :]
    out[0:1, T : 2 * T] = rbuf[1, 0:1, :]


def body(features, labels, label_table, tiles, tile_rows, tile_cols, tile_live, weights, gains, head_weight):
    vmem = pl.BlockSpec(memory_space=pltpu.VMEM)
    far = pl.BlockSpec(memory_space=pl.ANY)
    dma = pltpu.SemaphoreType.DMA
    return pl.pallas_call(
        kernel,
        out_shape=jax.ShapeDtypeStruct((1, 2 * T), F32),
        in_specs=[far] * 10,
        out_specs=vmem,
        scratch_shapes=[
            pltpu.VMEM((8, 256), I32),
            pltpu.VMEM((4, D), F32),
            pltpu.VMEM((8, SLOTS), I32),
            pltpu.VMEM((8, SLOTS), I32),
            pltpu.VMEM((1, 8), I32),
            pltpu.VMEM((1, D), BF16),
            pltpu.VMEM((1, D), F32),
            dma((7,)),
            pltpu.VMEM((2 * T, D), BF16),
            pltpu.VMEM((SLOTS, T, T), BF16),
            pltpu.VMEM((8, 256), I32),
            pltpu.VMEM((8, 256), I32),
            pltpu.VMEM((8, D), F32),
            pltpu.VMEM((LAYERS, 8, D), F32),
            pltpu.VMEM((LAYERS, D, D), BF16),
            pltpu.VMEM((4, 2 * T, D), BF16),
            pltpu.VMEM((2, T, D), BF16),
            pltpu.VMEM((2, 2 * T, D), BF16),
            pltpu.VMEM((2 * T, 2 * T), BF16),
            pltpu.VMEM((T, 3 * T), BF16),
            pltpu.VMEM((T, 2 * T), BF16),
            pltpu.VMEM((T, T), BF16),
            pltpu.VMEM((T, 3 * T), BF16),
            pltpu.VMEM((T, 3 * T), BF16),
            pltpu.VMEM((T, T), BF16),
            pltpu.VMEM((2 * T, D), F32),
            pltpu.VMEM((2 * T, D), F32),
            pltpu.VMEM((T, D), F32),
            pltpu.VMEM((T, D), BF16),
            pltpu.VMEM((2, 8, T), F32),
            pltpu.VMEM((2, 8, T), F32),
            dma((7,)),
            dma((7,)),
            dma,
            dma((3, QS)),
            dma((3,)),
            dma((LAYERS, QS)),
            dma((LAYERS,)),
            dma((QS,)),
            dma((1,)),
            dma((LAYERS, QS)),
            dma((LAYERS,)),
            dma,
            dma((2,)),
            dma((2,)),
            dma((2, 2)),
            dma((2, 2)),
            dma,
            dma,
        ],
        compiler_params=pltpu.CompilerParams(collective_id=0, has_side_effects=True),
    )(
        features, labels, label_table, tiles, tile_rows, tile_cols, tile_live.reshape(1, 8), weights, gains,
        head_weight.reshape(1, D),
    )


def solution(mesh):
    return jax.shard_map(
        body,
        mesh=mesh,
        in_specs=(
            P(None, "shard", None),
            P(None, "shard"),
            P(),
            P(None, "shard", None, None),
            P(None, "shard"),
            P(None, "shard"),
            P(None, "shard"),
            P("section", None, None),
            P("section", None),
            P(),
        ),
        out_specs=P("section", "shard"),
        check_vma=False,
    )
```

```python
import jax
import jax.numpy as jnp
from jax import lax
from jax.experimental import pallas as pl
from jax.experimental.pallas import tpu as pltpu
from jax.sharding import PartitionSpec as P

F32, BF16, I32 = jnp.float32, jnp.bfloat16, jnp.int32
T = 128
D = 512
Q = 128
QS = 4
LAYERS = 8
SLOTS = 6
YN = 4
XN = 4
CHAIN = 32
G1 = 2.0 * (2.0 / 3.141592653589793) ** 0.5
G3 = 4.0 * 0.044715 * G1


def dot(a, b):
    return jnp.dot(a, b, preferred_element_type=F32)


def remote(src, dst, send, recv, dev):
    return pltpu.make_async_remote_copy(
        src_ref=src,
        dst_ref=dst,
        send_sem=send,
        recv_sem=recv,
        device_id=dev,
        device_id_type=pl.DeviceIdType.MESH,
    )


def split(dev):
    sec, sh = dev
    return lax.div(sec, 2), lax.rem(sec, 2), lax.div(sh, XN), lax.rem(sh, XN)


def along(z, hi, f):
    return 2 * hi + jnp.where(lax.rem(z + hi, 2) == 0, f, 1 - f)


def work_of(dev):
    y, c, z, x = split(dev)
    hi, xl = lax.div(x, 2), lax.rem(x, 2)
    f = jnp.where(lax.rem(z + hi, 2) == 0, xl, 1 - xl)
    return 2 * y + hi, XN * z + 2 * f + c


def worker(dev):
    y, c, z, x = split(dev)
    return 2 * y + lax.rem(x, 2), XN * z + along(z, c, lax.div(x, 2))


def other_core(dev):
    y, c, z, x = split(dev)
    return 2 * y + 1 - c, dev[1]


def across(dev):
    y, c, z, x = split(dev)
    hi = lax.div(x, 2)
    place = lax.div(work_of(dev)[1], 2) + 2 * c - 1
    joined = (place >= 0) & (place < CHAIN)
    place = lax.rem(place + CHAIN, CHAIN)
    oz, of = lax.div(place, 2), lax.rem(place, 2)
    return (2 * y + 1 - c, XN * oz + along(oz, hi, of)), joined


def same(p, q):
    return (p[0] == q[0]) & (p[1] == q[1])


def kernel(
    feat, labels_h, table_h, tiles, rows_h, cols_h, live_h, w, gains_h, head_h,
    out,
    labels, table, rows, cols, live, gains, head, in_s,
    fbuf, tbuf, mown, mbuf, gown, gbuf, wbuf, sbuf, hs, hn, acat, pk, fk, rk, opk, npk, ain,
    emb, own, pre, hb,
    obuf, rbuf,
    red_s, red_r, wloc, os_s, gos_s, w_r, g_r, rel_s, grel_s, fw_s, gfw_s, t_s, h_s, h_r,
    n_s, n_r, o_s, o_r,
):
    sec = lax.axis_index("section")
    sh = lax.axis_index("shard")
    me = (sec, sh)
    y, c, z, x = split(me)
    sib = other_core(me)
    nb, joined = across(me)
    up = lax.rem(y + 1, YN)
    down = lax.rem(y + YN - 1, YN)
    opp = lax.rem(y + 2, YN)
    yp = (2 * up + c, sh)
    ym = (2 * down + c, sh)
    to = worker(me)
    to_sib = other_core(to)
    to_nb, to_joined = across(to)
    back, back_sib, back_nb = work_of(me), work_of(sib), work_of(nb)
    moves = jnp.logical_not(same(to, me))
    stay = same(to, me)
    rim_moves = jnp.logical_not(same(to_sib, me))
    far_moves = to_joined & jnp.logical_not(same(to_nb, me))
    far_stays = to_joined & same(to_nb, me)
    far_comes = joined & jnp.logical_not(same(back_nb, me))

    small = (
        (labels_h, labels), (rows_h, rows), (cols_h, cols), (live_h, live), (gains_h, gains),
        (table_h, table), (head_h, head),
    )
    fetches = [pltpu.make_async_copy(src, dst, in_s.at[i]) for i, (src, dst) in enumerate(small)]
    for fetch in fetches:
        fetch.start()
    get_tiles = pltpu.make_async_copy(tiles.at[sec], tbuf, t_s)
    get_tiles.start()

    barrier = pltpu.get_barrier_semaphore()

    def greet(*devs):
        for dev in devs:
            pl.semaphore_signal(barrier, inc=1, device_id=dev, device_id_type=pl.DeviceIdType.MESH)

    greet(sib, yp, ym)

    @pl.when(joined)
    def _():
        greet(nb)

    @pl.when(moves)
    def _():
        greet(to, back)

    @pl.when(rim_moves)
    def _():
        greet(to_sib, back_sib)

    @pl.when(far_moves)
    def _():
        greet(to_nb)

    @pl.when(far_comes)
    def _():
        greet(back_nb)

    for fetch in fetches:
        fetch.wait()

    mown[...] = jnp.broadcast_to(labels[pl.ds(sec, 1), :], (8, 256))
    gown[...] = jnp.broadcast_to(0.5 * gains[...].astype(F32), (8, D))
    amount = jnp.where(moves, 2, 0) + jnp.where(rim_moves, 2, 0) + jnp.where(far_moves, 1, 0)
    amount = amount + jnp.where(far_comes, 1, 0) + jnp.where(joined, 1, 0)
    pl.semaphore_wait(barrier, 3 + amount)

    tc = lax.rem(x, 2)
    fo, fi = pl.ds(pl.multiple_of(tc * T, T), T), pl.ds(pl.multiple_of((1 - tc) * T, T), T)
    red = (
        (mown, mbuf), (feat.at[sec, fo], fbuf.at[fo]), (feat.at[sec, fi], fbuf.at[fi]),
        (pk, opk), (fk, acat.at[pl.ds(0, T)]),
    )
    def part(q):
        return pl.ds(q * Q, Q)

    def own_weight(k, q, dev):
        return remote(w.at[0, part(q)], wbuf.at[sec, part(q)], os_s.at[k, q], w_r.at[sec, q], dev)

    def own_gain(k, dev):
        return remote(gown, gbuf.at[sec], gos_s.at[k], g_r.at[sec], dev)

    def forward(l, q, send, dev):
        return remote(wbuf.at[l, part(q)], wbuf.at[l, part(q)], send, w_r.at[l, q], dev)

    def forward_gain(l, send, dev):
        return remote(gbuf.at[l], gbuf.at[l], send, g_r.at[l], dev)

    def await_weight(l, q):
        pltpu.make_async_copy(wbuf.at[l, part(q)], wbuf.at[l, part(q)], w_r.at[l, q]).wait()

    def await_gain(l):
        pltpu.make_async_copy(gbuf.at[l], gbuf.at[l], g_r.at[l]).wait()

    lm, lp, l2 = 2 * down + c, 2 * up + c, 2 * opp + c

    def send_up(q):
        for k in (q, q + 1):
            own_weight(0, k, yp).start()

    def send_down(q):
        for k in (q, q + 1):
            own_weight(1, k, ym).start()

    def share(l, q):
        forward(l, q, fw_s.at[l, q], sib).start()

    def share_gain(l):
        forward_gain(l, gfw_s.at[l], sib).start()

    def relay(q):
        if q == 0:
            await_gain(lm)
            forward_gain(lm, grel_s.at[0], yp).start()
            share_gain(lm)
        await_weight(lm, q)
        forward(lm, q, rel_s.at[q], yp).start()
        await_weight(lp, q + 2)
        forward(lp, q + 2, rel_s.at[q + 2], ym).start()
        share(lm, q)
        share(lp, q + 2)

    def service(i):
        l = 2 * i + c

        @pl.when(i == down)
        def _():
            for q in (2, 3):
                await_weight(l, q)
                share(l, q)

        @pl.when(i == up)
        def _():
            await_gain(l)
            share_gain(l)
            for q in (0, 1):
                await_weight(l, q)
                share(l, q)

        @pl.when(i == opp)
        def _():
            await_gain(l)
            share_gain(l)
            for q in (0, 2, 1, 3):
                await_weight(l, q)
                share(l, q)

    own_local = pltpu.make_async_copy(w.at[0], wbuf.at[sec], wloc)
    own_local.start()
    gbuf[sec] = gown[...]

    own_gain(0, yp).start()
    own_gain(1, ym).start()
    send_up(0)
    send_down(2)

    late = (y == 2) | (c == 1)

    @pl.when((y != 1) & jnp.logical_not(late))
    def _():
        send_up(2)

    @pl.when((y != 3) & jnp.logical_not(late))
    def _():
        send_down(0)

    own_gain(2, sib).start()
    for q in range(QS):
        own_weight(2, q, sib).start()

    NPK, RIM = 5, 6

    def hand_over(some):
        @pl.when(moves)
        def _():
            for i in some:
                remote(*red[i], red_s.at[i], red_r.at[i], to).start()

        @pl.when(stay)
        def _():
            for i in some:
                pltpu.make_async_copy(*red[i], red_r.at[i]).start()

    hand_over((0, 1, 2))
    trow, tcol = rows[pl.ds(sec, 1), :], cols[pl.ds(sec, 1), :]
    lane = lax.broadcasted_iota(I32, (1, 8), 1)
    tlive = jnp.sum(jnp.where(lane == sec, live[...], 0), axis=1, keepdims=True)
    alive = lax.broadcasted_iota(I32, (1, SLOTS), 1) < tlive
    get_tiles.wait()

    def dense(r, cc):
        coef = jnp.where((trow == r) & (tcol == cc) & alive, 1.0, 0.0).astype(F32)
        total = coef[:, 0:1] * tbuf[0].astype(F32)
        for k in range(1, SLOTS):
            total = total + coef[:, k : k + 1] * tbuf[k].astype(F32)
        return total.astype(BF16)

    inner, outer = 2 * sh + 1 - tc, 2 * sh + tc
    pk[:, 0:T] = dense(outer, inner)
    pk[:, T : 2 * T] = dense(outer, outer)
    pk[:, 2 * T : 3 * T] = dense(2 * sh - 1 + 3 * tc, outer)
    fk[:, 0:T] = dense(inner, inner)
    fk[:, T : 2 * T] = dense(inner, outer)
    rk[...] = dense(2 * sh + 2 - 3 * tc, inner)

    hand_over((3, 4))

    give_far = remote(pk, npk, red_s.at[NPK], red_r.at[NPK], to_nb)
    give_rim = remote(rk, ain, red_s.at[RIM], red_r.at[RIM], to_sib)

    @pl.when(far_moves)
    def _():
        give_far.start()

    @pl.when(far_stays)
    def _():
        pltpu.make_async_copy(pk, npk, red_r.at[NPK]).start()

    @pl.when(rim_moves)
    def _():
        give_rim.start()

    @pl.when(jnp.logical_not(rim_moves))
    def _():
        pltpu.make_async_copy(rk, ain, red_r.at[RIM]).start()

    def await_red(i, dst):
        pltpu.make_async_copy(dst, dst, red_r.at[i]).wait()

    @pl.when(jnp.logical_not(joined))
    def _():
        npk[...] = jnp.zeros((T, 3 * T), BF16)
        hn[...] = jnp.zeros((2, 2 * T, D), BF16)

    inn, out_ = pl.ds(0, T), pl.ds(T, T)

    def send_inner(level):
        k = lax.rem(level, 2)
        return remote(sbuf.at[lax.rem(level, 4), inn], hs.at[k], h_s.at[k], h_r.at[k], sib)

    def send_across(step, p):
        k = lax.rem(step, 2)
        rs = pl.ds(p * T, T)
        return remote(sbuf.at[2 * k, rs], hn.at[k, rs], n_s.at[k, p], n_r.at[k, p], nb)

    def cross(step, p, what):
        @pl.when(joined)
        def _():
            if what == "go":
                send_across(step, p).start()
            else:
                send_across(step, p).wait()

    await_red(0, mbuf)
    kinds = lax.broadcasted_iota(I32, (T, 256), 0)
    hot = jnp.where(kinds == mbuf[0:1, :], 1.0, 0.0).astype(F32).T
    embedded = hot[:, 0:1] * table[0:1, :]
    for k in range(1, 4):
        embedded = embedded + hot[:, k : k + 1] * table[k : k + 1, :]
    emb[...] = embedded

    ro, ri = pl.ds(pl.multiple_of(c * T, T), T), pl.ds(pl.multiple_of((1 - c) * T, T), T)
    await_red(1, fbuf.at[ro])

    @pl.when((y != 1) & late)
    def _():
        send_up(2)

    @pl.when((y != 3) & late)
    def _():
        send_down(0)

    sbuf[0, out_, :] = (fbuf[ro, :].astype(F32) + emb[ro, :]).astype(BF16)
    cross(0, 1, "go")
    relay(0)
    await_red(2, fbuf.at[ri])
    sbuf[0, inn, :] = (fbuf[ri, :].astype(F32) + emb[ri, :]).astype(BF16)
    cross(0, 0, "go")
    send_inner(0).start()
    relay(1)

    @pl.when(y == 1)
    def _():
        send_up(2)

    @pl.when(y == 3)
    def _():
        send_down(0)

    await_red(3, opk)
    await_red(4, acat.at[pl.ds(0, T)])
    acat[T : 2 * T, :] = opk[:, 0 : 2 * T]
    service(0)
    own_local.wait()
    await_red(RIM, ain)

    @pl.when(joined)
    def _():
        await_red(NPK, npk)

    def other_weight(l):
        await_gain(l)
        for q in range(QS):
            await_weight(l, q)

    def update(l, aggregate, before):
        projected = dot(aggregate.astype(BF16), wbuf[l])
        scale = lax.rsqrt(jnp.mean(projected * projected, axis=-1, keepdims=True) + 1e-6)
        h = (projected * scale) * gbuf[l][0:1, :]
        gate = jnp.tanh(h * (G1 + G3 * (h * h)))
        return (before.astype(F32) + (h + h * gate)).astype(BF16)

    def two_layers(i, k, final):
        l = 2 * i
        a, b, n = 2 * k, 2 * k + 1, 2 - 2 * k

        def go(p):
            if final is None:
                cross(i + 1, p, "go")
                if p == 0:
                    send_inner(l + 2).start()
            else:
                @pl.when(final)
                def _():
                    cross(i + 1, p, "go")
                    if p == 0:
                        send_inner(l + 2).start()

        def near_outer():
            sbuf[b, out_, :] = update(
                l, own[out_, :] + dot(npk[:, 2 * T : 3 * T], hn[k, out_, :]), sbuf[a, out_, :]
            )

        def far_outer(sl, p):
            hb[...] = update(l, pre[...] + dot(npk[:, sl], hn[k, p, :]), hn[k, out_, :])

        def both_outer():
            tiles2 = jnp.concatenate([npk[:, 2 * T : 3 * T], npk[:, T : 2 * T]], axis=0)
            received = hn[k, out_, :]
            more = dot(tiles2, received)
            aggregate = more + jnp.concatenate([own[out_, :], pre[...]], axis=0)
            new = update(l, aggregate, jnp.concatenate([sbuf[a, out_, :], received], axis=0))
            sbuf[b, out_, :] = new[0:T]
            hb[...] = new[T : 2 * T]

        def next_inner():
            sbuf[n, inn, :] = update(
                l + 1, dot(acat[inn, :], sbuf[b]) + dot(ain[...], hs[1]), sbuf[b, inn, :]
            )
            go(0)

        def next_outer():
            sbuf[n, out_, :] = update(
                l + 1, dot(acat[out_, :], sbuf[b]) + dot(npk[:, 2 * T : 3 * T], hb[...]), sbuf[b, out_, :]
            )
            go(1)

        own[...] = dot(acat[...], sbuf[a])

        @pl.when(c == 1)
        def _():
            other_weight(l)

        send_inner(l).wait()
        sbuf[b, inn, :] = update(l, own[inn, :] + dot(ain[...], hs[0]), sbuf[a, inn, :])
        send_inner(l + 1).start()

        def second_weight():
            @pl.when(c == 0)
            def _():
                other_weight(l + 1)

        left, right = slice(0, T), slice(T, 2 * T)
        if k == 0:
            cross(i, 0, "take")
            pre[...] = dot(opk[:, 2 * T : 3 * T], sbuf[a, out_, :]) + dot(npk[:, left], hn[k, inn, :])
            cross(i, 1, "take")
            both_outer()
            second_weight()
            next_outer()
            send_inner(l + 1).wait()
            next_inner()
        else:
            cross(i, 1, "take")
            near_outer()
            second_weight()
            send_inner(l + 1).wait()
            next_inner()
            pre[...] = dot(opk[:, 2 * T : 3 * T], sbuf[a, out_, :]) + dot(npk[:, right], hn[k, out_, :])
            cross(i, 0, "take")
            far_outer(left, inn)
            next_outer()

    def four_layers(j, carry):
        two_layers(2 * j, 0, None)
        service(2 * j + 1)
        two_layers(2 * j + 1, 1, j < LAYERS // 4 - 1)

        @pl.when(j < LAYERS // 4 - 1)
        def _():
            service(2 * j + 2)

        return carry

    lax.fori_loop(0, LAYERS // 4, four_layers, 0)

    last = sbuf[0]
    weight = jnp.broadcast_to(head[...], (8, D))
    top = weight.astype(BF16)
    rest = weight - top.astype(F32)
    mid = rest.astype(BF16)
    low = (rest - mid.astype(F32)).astype(BF16)

    def against(part):
        return lax.dot_general(part, last, (((1,), (1,)), ((), ())), preferred_element_type=F32)

    result = against(top) + against(mid) + against(low)
    obuf[1 - c] = result[:, 0:T]
    obuf[c] = result[:, T : 2 * T]

    @pl.when(moves)
    def _():
        give = remote(obuf, rbuf, o_s, o_r, back)
        give.start()
        give.wait_send()

    @pl.when(stay)
    def _():
        pltpu.make_async_copy(obuf, rbuf, o_r).start()

    for k, dev in enumerate((yp, ym, sib)):
        own_gain(k, dev).wait_send()

    for k, dev in enumerate((yp, ym, sib)):
        for q in range(QS):
            own_weight(k, q, dev).wait_send()

    forward_gain(lm, grel_s.at[0], yp).wait_send()
    for q in (0, 1):
        forward(lm, q, rel_s.at[q], yp).wait_send()
        forward(lp, q + 2, rel_s.at[q + 2], ym).wait_send()
    for l in (lm, lp, l2):
        forward_gain(l, gfw_s.at[l], sib).wait_send()
        for q in range(QS):
            forward(l, q, fw_s.at[l, q], sib).wait_send()

    @pl.when(moves)
    def _():
        for i, (src, dst) in enumerate(red):
            remote(src, dst, red_s.at[i], red_r.at[i], to).wait_send()

    @pl.when(far_moves)
    def _():
        give_far.wait_send()

    @pl.when(rim_moves)
    def _():
        give_rim.wait_send()

    pltpu.make_async_copy(rbuf, rbuf, o_r).wait()
    out[0:1, 0:T] = rbuf[0, 0:1, :]
    out[0:1, T : 2 * T] = rbuf[1, 0:1, :]


def body(features, labels, label_table, tiles, tile_rows, tile_cols, tile_live, weights, gains, head_weight):
    vmem = pl.BlockSpec(memory_space=pltpu.VMEM)
    far = pl.BlockSpec(memory_space=pl.ANY)
    dma = pltpu.SemaphoreType.DMA
    return pl.pallas_call(
        kernel,
        out_shape=jax.ShapeDtypeStruct((1, 2 * T), F32),
        in_specs=[far] * 10,
        out_specs=vmem,
        scratch_shapes=[
            pltpu.VMEM((8, 256), I32),
            pltpu.VMEM((4, D), F32),
            pltpu.VMEM((8, SLOTS), I32),
            pltpu.VMEM((8, SLOTS), I32),
            pltpu.VMEM((1, 8), I32),
            pltpu.VMEM((1, D), BF16),
            pltpu.VMEM((1, D), F32),
            dma((7,)),
            pltpu.VMEM((2 * T, D), BF16),
            pltpu.VMEM((SLOTS, T, T), BF16),
            pltpu.VMEM((8, 256), I32),
            pltpu.VMEM((8, 256), I32),
            pltpu.VMEM((8, D), F32),
            pltpu.VMEM((LAYERS, 8, D), F32),
            pltpu.VMEM((LAYERS, D, D), BF16),
            pltpu.VMEM((4, 2 * T, D), BF16),
            pltpu.VMEM((2, T, D), BF16),
            pltpu.VMEM((2, 2 * T, D), BF16),
            pltpu.VMEM((2 * T, 2 * T), BF16),
            pltpu.VMEM((T, 3 * T), BF16),
            pltpu.VMEM((T, 2 * T), BF16),
            pltpu.VMEM((T, T), BF16),
            pltpu.VMEM((T, 3 * T), BF16),
            pltpu.VMEM((T, 3 * T), BF16),
            pltpu.VMEM((T, T), BF16),
            pltpu.VMEM((2 * T, D), F32),
            pltpu.VMEM((2 * T, D), F32),
            pltpu.VMEM((T, D), F32),
            pltpu.VMEM((T, D), BF16),
            pltpu.VMEM((2, 8, T), F32),
            pltpu.VMEM((2, 8, T), F32),
            dma((7,)),
            dma((7,)),
            dma,
            dma((3, QS)),
            dma((3,)),
            dma((LAYERS, QS)),
            dma((LAYERS,)),
            dma((QS,)),
            dma((1,)),
            dma((LAYERS, QS)),
            dma((LAYERS,)),
            dma,
            dma((2,)),
            dma((2,)),
            dma((2, 2)),
            dma((2, 2)),
            dma,
            dma,
        ],
        compiler_params=pltpu.CompilerParams(collective_id=0, has_side_effects=True),
    )(
        features, labels, label_table, tiles, tile_rows, tile_cols, tile_live.reshape(1, 8), weights, gains,
        head_weight.reshape(1, D),
    )


def solution(mesh):
    return jax.shard_map(
        body,
        mesh=mesh,
        in_specs=(
            P(None, "shard", None),
            P(None, "shard"),
            P(),
            P(None, "shard", None, None),
            P(None, "shard"),
            P(None, "shard"),
            P(None, "shard"),
            P("section", None, None),
            P("section", None),
            P(),
        ),
        out_specs=P("section", "shard"),
        check_vma=False,
    )
```
